512 devices in a mesh: rows: 64 (over y, x, core), cols: 8 (over z).
Axes of the slice: x: 4, y: 8, z: 8, core: 2. Of those that a mesh axis runs over, the one named last changes fastest.
Arguments:
- fact_cells: bfloat16 [3072, 32, 512], P('rows', 'cols'), may hold values from -6 to 6
- gain_col: float32 [512], replicated, may hold values from 0.1 to 1.9
- w_qkv: bfloat16 [512, 1536], replicated, may hold values from -0.25 to 0.25
- w_col_out: bfloat16 [512, 512], replicated, may hold values from -0.25 to 0.25
- gain_tile: float32 [512], replicated, may hold values from 0.1 to 1.9
- w_query: bfloat16 [512, 512], replicated, may hold values from -0.25 to 0.25
- w_tile_out: bfloat16 [512, 512], replicated, may hold values from -0.25 to 0.25
- tile_kv: bfloat16 [256, 128, 8, 128], P('rows', None, 'cols'), may hold values from -70 to 70
- tile_ids: int32 [64, 48], P('rows'), may hold values from -1 to 255, as said below
- key_mask: int32 [3072, 48], P('rows'), may hold values from 0 to 1, as said below
Outputs:
- layer_out: bfloat16 [3072, 32, 512], P('rows', 'cols')
The draws below stay inside these ranges and needn't reach their ends.
Inputs may be any that keep to these rules, and one draw needn't show every extreme that they name: `tile_ids`: tile t is held by index t // 4 of rows. In every block the first slots, 36 of them or more, hold distinct tile ids and the rest hold -1; some block fills all 48 slots. The listed tiles of one block are held by distinct indices of rows. `key_mask`: 0 wherever the row's block holds -1 in that slot; 1 in slot 0 of every row.
All inputs are finite; a program needn't handle non-finite values.
Results may differ from the reference program's by a relative error of at most 0.023.
The reference program's roundings to bfloat16 on the way (of `normed`, `packed`, `col_weights`, `mixed_col`, `normed2`, `asked_q`, `tile_weights` and `answer`) count: a program that leaves them out, or rounds other values in their place, can miss the bound.
Values may be sent and summed in bfloat16 or wider, within the bound.
A program may use at most 64 MiB of HBM per device.

```python
import jax
import jax.numpy as jnp
from jax import lax

D = 512
HEADS = 8
HD = 64
COLUMNS = 32
R_DEV = 48
ROWS = 3072
BLOCKS = 64
KEYS = 128
TILE_DEV = 4
NTILES = 256
CAP = 1
MAXT = 48


def count_draw(key):
    base_key = jax.random.fold_in(key, 11)
    key_first, key_second = jax.random.split(base_key)
    block_counts = jax.random.randint(key_first, (BLOCKS,), 3 * MAXT // 4, MAXT + 1)
    full_block = jax.random.randint(key_second, (), 0, BLOCKS)
    return jnp.where(jnp.arange(BLOCKS) == full_block, MAXT, block_counts).astype(jnp.int32)


def ids_block(block_key, block_count):
    key_perm, key_offs, key_order = jax.random.split(block_key, 3)
    slot_total = BLOCKS * CAP
    perm_order = jax.random.permutation(key_perm, slot_total)
    partner = (perm_order[0] + BLOCKS) % slot_total
    where_partner = jnp.argmax(perm_order == partner)
    second_val = perm_order[1]
    perm_order = perm_order.at[1].set(partner)
    perm_order = perm_order.at[where_partner].set(second_val)
    picked = perm_order[:MAXT]
    owners = picked % BLOCKS
    copies = picked // BLOCKS
    offsets = jax.random.randint(key_offs, (BLOCKS,), 0, TILE_DEV)
    local_idx = (offsets[owners] + copies) % TILE_DEV
    tile_list = owners * TILE_DEV + local_idx
    slot_pos = jnp.arange(MAXT)
    order_scores = jnp.where(slot_pos < block_count, jax.random.permutation(key_order, MAXT), MAXT + slot_pos)
    shuffle_idx = jnp.argsort(order_scores)
    return jnp.where(slot_pos < block_count, tile_list[shuffle_idx], -1).astype(jnp.int32)


def draw_tile_ids(key, part):
    block_counts = count_draw(key)
    block_keys = jax.random.split(jax.random.fold_in(key, 23), BLOCKS)
    return jax.vmap(ids_block)(block_keys, block_counts)


def draw_key_mask(key, part):
    block_counts = count_draw(key)
    mask_bits = jax.random.randint(jax.random.fold_in(key, 37), (ROWS, MAXT), 0, 2)
    slot_pos = jnp.arange(MAXT)[None, :]
    row_count = jnp.repeat(block_counts, R_DEV)[:, None]
    live_slot = (slot_pos < row_count).astype(jnp.int32)
    return (jnp.where(slot_pos == 0, 1, mask_bits) * live_slot).astype(jnp.int32)


def draw_tile_kv(key, part):
    key_a, key_b = jax.random.split(key, 2)
    arr_shape = (NTILES, KEYS, HEADS, HD)
    key_part = 2.0 * jax.random.normal(key_a, arr_shape, jnp.float32)
    val_part = 3.0 * jax.random.normal(key_b, arr_shape, jnp.float32)
    return jnp.concatenate([key_part, val_part], axis=-1).astype(jnp.bfloat16)


def steps_of(own_key, extent, shards, least, high):
    gain = 1.0
    for dim, parts in shards:
        draws = jax.random.uniform(jax.random.fold_in(jax.random.fold_in(own_key, 6), dim), (parts,), jnp.float32, least / len(shards), high / len(shards))
        gain = gain * jnp.repeat(jnp.exp(draws), extent[dim] // parts).reshape((-1,) + (1,) * (len(extent) - 1 - dim))
    return gain


def normal_values(key, dims, scale, bound, cuts=(), held_as=jnp.bfloat16):
    level = steps_of(key, dims, cuts, -0.22, 0.18) if cuts else 1.0
    entries = jax.random.normal(key, dims, jnp.float32) * scale * level
    return jnp.minimum(jnp.maximum(entries, -bound), bound).astype(held_as)


def setup_inputs(seed: int = 0) -> dict:
    seeds = jax.random.split(jax.random.key(seed), 11)
    return {
        "fact_cells": normal_values(seeds[0], (ROWS, COLUMNS, D), 1.0, 6.0, ((0, 64), (1, 8))),
        "gain_col": jnp.clip(1.0 + 0.18 * jax.random.normal(seeds[1], (D,), jnp.float32), 0.1, 1.9),
        "w_qkv": normal_values(seeds[2], (D, 3 * D), D ** -0.5, 0.25),
        "w_col_out": normal_values(seeds[3], (D, D), D ** -0.5, 0.25),
        "gain_tile": jnp.clip(1.0 + 0.18 * jax.random.normal(seeds[4], (D,), jnp.float32), 0.1, 1.9),
        "w_query": normal_values(seeds[5], (D, D), D ** -0.5, 0.25),
        "w_tile_out": normal_values(seeds[6], (D, D), D ** -0.5, 0.25),
        "tile_kv": draw_tile_kv(jax.random.fold_in(seeds[10], 71), 0),
        "tile_ids": draw_tile_ids(jax.random.fold_in(seeds[10], 71), 0),
        "key_mask": draw_key_mask(jax.random.fold_in(seeds[10], 71), 0),
    }


def rms_scale(values, gain_vec):
    mean_sq = lax.optimization_barrier(jnp.mean(values * values, axis=-1, keepdims=True))
    return values * lax.rsqrt(mean_sq + 1e-05) * gain_vec

def soft_weights(scores, axes):
    row_top = lax.optimization_barrier(jnp.max(scores, axis=axes, keepdims=True))
    expo_vals = jnp.exp(scores - row_top)
    return expo_vals / lax.optimization_barrier(jnp.sum(expo_vals, axis=axes, keepdims=True))

def rounded(values):
    return lax.optimization_barrier(values.astype(jnp.bfloat16)).astype(jnp.float32)

def reference(fact_cells, gain_col, w_qkv, w_col_out, gain_tile, w_query, w_tile_out, tile_kv, tile_ids, key_mask):
    row_total, col_total, model_width = fact_cells.shape
    head_size = model_width // HEADS
    scale = head_size ** (-0.5)
    residual = fact_cells.astype(jnp.float32)
    normed = rms_scale(residual, gain_col).astype(jnp.bfloat16)
    packed = jnp.dot(normed.reshape(-1, model_width), w_qkv, preferred_element_type=jnp.float32)
    packed = rounded(packed).reshape(row_total, col_total, 3, HEADS, head_size)
    queries = packed[:, :, 0]
    key_part = packed[:, :, 1]
    val_part = packed[:, :, 2]
    scores = jnp.einsum('rchd,rkhd->rhck', queries, key_part) * scale
    col_weights = rounded(soft_weights(scores, (3,)))
    mixed_col = jnp.einsum('rhck,rkhd->rchd', col_weights, val_part).astype(jnp.bfloat16)
    residual2 = residual + jnp.dot(mixed_col.reshape(-1, model_width), w_col_out, preferred_element_type=jnp.float32).reshape(residual.shape)
    normed2 = rms_scale(residual2, gain_tile).astype(jnp.bfloat16)
    asked_q = jnp.dot(normed2.reshape(-1, model_width), w_query, preferred_element_type=jnp.float32)
    asked_q = rounded(asked_q).reshape(row_total, col_total, HEADS, head_size)

    def one_block(block_idx):
        start = block_idx * 4
        block_q = lax.dynamic_slice_in_dim(asked_q, start, 4, 0)
        block_m = lax.dynamic_slice_in_dim(key_mask, start, 4, 0)
        slot_ids = lax.dynamic_index_in_dim(tile_ids, start // R_DEV, 0, keepdims=False)
        chosen = jnp.take(tile_kv, jnp.maximum(slot_ids, 0).astype(jnp.int32), axis=0).astype(jnp.float32)
        tile_keys = chosen[..., :head_size]
        tile_vals = chosen[..., head_size:]
        block_scores = jnp.einsum('rchd,tkhd->rchtk', block_q, tile_keys) * scale
        live_keys = (block_m > 0)[:, None, None, :, None]
        block_scores = jnp.where(live_keys, block_scores, -1e+30)
        tile_weights = rounded(soft_weights(block_scores, (3, 4)))
        return jnp.einsum('rchtk,tkhd->rchd', tile_weights, tile_vals).astype(jnp.bfloat16)
    answer = lax.map(one_block, jnp.arange(row_total // 4, dtype=jnp.int32))
    answer = answer.reshape(row_total * col_total, model_width)
    layer_out = residual2 + jnp.dot(answer, w_tile_out, preferred_element_type=jnp.float32).reshape(residual.shape)
    return layer_out.astype(jnp.bfloat16)
```

```python
import functools
import math

import jax
import jax.numpy as jnp
from jax import lax
from jax.experimental import pallas as pl
from jax.experimental.pallas import tpu as pltpu
from jax.sharding import PartitionSpec as P

F32, BF = jnp.float32, jnp.bfloat16
MESH = pl.DeviceIdType.MESH
NT = (((1,), (1,)), ((), ()))
ZN = 8
GROUP = 24
CELLS = ZN * GROUP
D = 512
PLANE = 8
STEPS = ((0, 0), (1, 1), (-1, 5), (2, 2), (-2, 6), (3, 3), (-3, 7), (4, 4))


def rms(values, gain):
    mean_sq = jnp.mean(values * values, axis=-1, keepdims=True)
    return (values * lax.rsqrt(mean_sq + 1e-05) * gain).astype(BF)


def row_of(shape, dim):
    return (lax.broadcasted_iota(jnp.int32, shape, dim) % GROUP) >> 2


def layer_kernel(
    rows_n,
    maxt,
    ids_ref,
    mask_ref,
    fact_ref,
    gain_col_ref,
    gain_tile_ref,
    tile_ref,
    w_qkv_hbm,
    w_col_hbm,
    w_query_hbm,
    w_out_hbm,
    out_ref,
    xin,
    packed_buf,
    delta_send,
    delta_buf,
    q_send,
    q_buf,
    o_send,
    a_buf,
    y1,
    y2,
    y3,
    y4,
    y5,
    y6,
    y7,
    x_send,
    kv_buf,
    k_all,
    v_all,
    my_list,
    lists,
    lists_s,
    w_qkv,
    w_col,
    w_query,
    w_pad,
    w_sem,
    list_sem,
    cell_ss,
    cell_rs,
    list_ss,
    list_rs,
    delta_ss,
    delta_rs,
    q_ss,
    q_rs,
    o_ss,
    o_rs,
    y_ss,
    y_rs,
    x_ss,
    x_rs,
):
    row = lax.axis_index("rows")
    me = lax.axis_index("cols")
    seat = lax.rem(row, PLANE)
    base = row - seat

    def at_z(k):
        return lax.rem(me + k, ZN)

    def at_seat(d):
        return base + lax.rem(seat + d, PLANE)

    def at_y(dy):
        return lax.rem(row + dy * PLANE + rows_n, rows_n)

    def to_z(src, dst, ss, rs, k):
        return pltpu.make_async_remote_copy(
            src, dst, ss, rs, device_id=(row, at_z(k)), device_id_type=MESH
        )

    def to_row(src, dst, ss, rs, r):
        return pltpu.make_async_remote_copy(src, dst, ss, rs, device_id=(r, me), device_id_type=MESH)

    w_copies = [
        pltpu.make_async_copy(w_qkv_hbm, w_qkv, w_sem.at[0]),
        pltpu.make_async_copy(w_col_hbm, w_col, w_sem.at[1]),
        pltpu.make_async_copy(w_query_hbm, w_query, w_sem.at[2]),
    ] + [
        pltpu.make_async_copy(
            w_out_hbm.at[pl.ds(64 * h, 64)], w_pad.at[pl.ds(128 * h + 64, 64)], w_sem.at[3 + h]
        )
        for h in range(ZN)
    ]
    for copy in w_copies:
        copy.start()

    barrier = pltpu.get_barrier_semaphore()

    @pl.loop(1, ZN)
    def _(k):
        pl.semaphore_signal(barrier, inc=1, device_id=(row, at_z(k)), device_id_type=MESH)
        pl.semaphore_signal(barrier, inc=1, device_id=(at_seat(k), me), device_id_type=MESH)

    for dy in (1, -1):
        pl.semaphore_signal(barrier, inc=1, device_id=(at_y(dy), me), device_id_type=MESH)

    lane8 = lax.broadcasted_iota(jnp.int32, (8, 128), 1)
    picks = jnp.zeros((8, 128), jnp.int32)
    for j in range(maxt):
        slot_id = ids_ref[0, j]
        picks = jnp.where(lane8 == (slot_id >> 2), slot_id & 3, picks)
    my_list[...] = picks
    lists[0] = picks
    for h in range(ZN):
        w_pad[pl.ds(128 * h, 64), :] = jnp.zeros((64, D), BF)

    pl.semaphore_wait(barrier, 16)

    @pl.loop(1, ZN)
    def _(k):
        to_z(fact_ref.at[at_z(k)], xin.at[me], cell_ss.at[k], cell_rs.at[k], k).start()
        to_row(my_list, lists.at[k], list_ss.at[k], list_rs.at[k], at_seat(k)).start()

    y_bufs = (None, y1, y2, y3, y4, y5, y6, y7)
    y_copies = []

    def y_forward(src, number, sign):
        copy = to_row(
            src,
            y_bufs[number + 1 if sign > 0 else number - 4 + 5],
            y_ss.at[number],
            y_rs.at[number],
            at_y(sign),
        )
        copy.start()
        y_copies.append(copy)

    y_forward(tile_ref, 0, 1)
    y_forward(tile_ref, 4, -1)
    xin[me] = fact_ref[me]

    @pl.loop(1, PLANE)
    def _(k):
        to_row(my_list, lists.at[k], list_ss.at[k], list_rs.at[k], at_seat(k)).wait()

    list_copy = pltpu.make_async_copy(lists, lists_s, list_sem)
    list_copy.start()
    list_copy.wait()

    def x_copy(s, d, owner):
        return to_row(
            x_send.at[s, d], kv_buf.at[owner], x_ss.at[s, d], x_rs.at[s, d], at_seat(d)
        )

    def hand_out(s, dy, src):
        owner = at_y(-dy)
        kv_buf[owner] = src[lists_s[0, 0, owner]]

        @pl.loop(1, PLANE)
        def _(d):
            x_send[s, d] = src[lists_s[PLANE - d, 0, owner]]
            x_copy(s, d, owner).start()

    def relay(s):
        dy, number = STEPS[s]
        buf = y_bufs[number]
        sem = number - 1
        to_row(buf, buf, y_ss.at[sem], y_rs.at[sem], at_y(1)).wait_recv()
        if dy > 0 and dy < 4:
            y_forward(buf, number, 1)
        if dy < 0 and dy > -3:
            y_forward(buf, number, -1)
        hand_out(s, dy, buf)

    hand_out(0, 0, tile_ref)

    @pl.loop(1, ZN)
    def _(k):
        to_z(fact_ref.at[at_z(k)], xin.at[me], cell_ss.at[k], cell_rs.at[k], k).wait()

    x = xin[...].astype(F32).reshape(CELLS, D)
    normed = rms(x, gain_col_ref[...])
    w_copies[0].wait()
    packed_buf[...] = jnp.dot(normed, w_qkv[...], preferred_element_type=F32).astype(BF)
    relay(1)
    relay(2)

    same_row = row_of((CELLS, CELLS), 0) == row_of((CELLS, CELLS), 1)
    low = lax.broadcasted_iota(jnp.int32, (CELLS, 128), 1) < 64
    mixed = []
    for pair in range(4):
        q2 = packed_buf[:, pl.ds(128 * pair, 128)]
        k2 = packed_buf[:, pl.ds(D + 128 * pair, 128)]
        v2 = packed_buf[:, pl.ds(2 * D + 128 * pair, 128)]
        parts = []
        for half in range(2):
            q1 = jnp.where(low if half == 0 else ~low, q2, jnp.zeros_like(q2))
            s = lax.dot_general(q1, k2, NT, preferred_element_type=F32) * 0.125
            s = jnp.where(same_row, s, -1e30)
            e = jnp.exp(s - jnp.max(s, axis=1, keepdims=True))
            w = (e / jnp.sum(e, axis=1, keepdims=True)).astype(BF)
            parts.append(jnp.dot(w, v2, preferred_element_type=F32))
        mixed.append(jnp.where(low, parts[0], parts[1]).astype(BF))
    mixed = jnp.concatenate(mixed, axis=1)
    w_copies[1].wait()
    delta = jnp.dot(mixed, w_col[...], preferred_element_type=F32)
    relay(3)
    relay(4)
    normed2 = rms(x + delta, gain_tile_ref[...])
    w_copies[2].wait()
    asked = jnp.dot(normed2, w_query[...], preferred_element_type=F32)
    asked = asked * (0.125 * math.log2(math.e))
    low96 = lax.broadcasted_iota(jnp.int32, (CELLS // 2, 128), 1) < 64
    for pair in range(4):
        top = asked[: CELLS // 2, 128 * pair : 128 * pair + 128]
        bot = asked[CELLS // 2 :, 128 * pair : 128 * pair + 128]
        q_send[2 * pair] = jnp.where(low96, top, pltpu.roll(bot, 64, 1)).astype(BF)
        q_send[2 * pair + 1] = jnp.where(low96, pltpu.roll(top, 64, 1), bot).astype(BF)
    delta_send[...] = delta.reshape(ZN, GROUP, D).astype(BF)
    q_buf[me] = q_send[me]
    delta_buf[me] = delta_send[me]

    def q_copy(k):
        return to_z(q_send.at[at_z(k)], q_buf.at[me], q_ss.at[k], q_rs.at[k], k)

    def delta_copy(k):
        return to_z(delta_send.at[at_z(k)], delta_buf.at[me], delta_ss.at[k], delta_rs.at[k], k)

    @pl.loop(1, ZN)
    def _(k):
        q_copy(k).start()

    @pl.loop(1, ZN)
    def _(k):
        delta_copy(k).start()

    for s in range(5, 8):
        relay(s)

    for s, (dy, _number) in enumerate(STEPS):

        @pl.loop(1, PLANE)
        def _(d):
            x_copy(s, d, at_y(-dy)).wait_recv()

    lane = lax.broadcasted_iota(jnp.int32, (128, 128), 1)

    @pl.loop(0, maxt)
    def _(j):
        kv = kv_buf[jnp.maximum(ids_ref[0, j], 0) >> 2].astype(F32)
        at = pl.ds(pl.multiple_of(j * 128, 128), 128)
        k_all[at, :] = jnp.where(lane < 64, kv, jnp.where(lane == 64 + j, 1.0, 0.0)).astype(BF)
        v_all[at, :] = jnp.where(lane < 64, jnp.where(lane == 0, 1.0, 0.0), kv).astype(BF)

    @pl.loop(1, ZN)
    def _(k):
        q_copy(k).wait()

    dead = jnp.where(mask_ref[...] > 0, 0.0, -1e30)
    rows_dev = dead.shape[0]
    dead = jnp.concatenate(
        [jnp.zeros((rows_dev, 64), F32), dead, jnp.zeros((rows_dev, 64 - maxt), F32)], axis=1
    ).astype(BF)

    def o_copy(z, k):
        return to_z(
            o_send.at[z, at_z(k)], a_buf.at[me, z], o_ss.at[z, k], o_rs.at[z, k], k
        )

    @pl.loop(0, ZN)
    def _(z):
        mine = z * 6 + row_of((CELLS, rows_dev), 0)
        pick = jnp.where(lax.broadcasted_iota(jnp.int32, (CELLS, rows_dev), 1) == mine, 1.0, 0.0)
        bias = jnp.dot(pick.astype(BF), dead, preferred_element_type=F32)
        q = q_buf[z].astype(F32)
        q = jnp.concatenate(
            [
                jnp.where(low96, q, bias[: CELLS // 2]),
                jnp.where(low96, pltpu.roll(q, 64, 1), bias[CELLS // 2 :]),
            ],
            axis=0,
        ).astype(BF)
        s = lax.dot_general(q, k_all[...], NT, preferred_element_type=F32)
        p = jnp.exp2(s - jnp.max(s, axis=1, keepdims=True)).astype(BF)
        o = jnp.dot(p, v_all[...], preferred_element_type=F32)
        o = o / o[:, 0:1]
        o_send[z] = o.reshape(ZN, GROUP, 128).astype(BF)
        a_buf[me, z] = o_send[z, me]

        @pl.loop(1, ZN)
        def _(k):
            o_copy(z, k).start()

    for copy in w_copies[3:]:
        copy.wait()

    @pl.loop(1, ZN)
    def _(k):
        delta_copy(k).wait()

    base_cells = fact_ref[...].astype(F32).reshape(CELLS, D) + delta_buf[...].astype(
        F32
    ).reshape(CELLS, D)

    @pl.loop(0, ZN)
    def _(z):
        @pl.loop(1, ZN)
        def _(k):
            o_copy(z, k).wait()

    answer = jnp.concatenate(
        [a_buf[h].astype(F32).reshape(CELLS, 128).astype(BF) for h in range(ZN)], axis=1
    )
    final = base_cells + jnp.dot(answer, w_pad[...], preferred_element_type=F32)
    out_ref[...] = final.reshape(ZN, GROUP, D).astype(BF)

    for copy in y_copies:
        copy.wait_send()
    for s, (dy, _number) in enumerate(STEPS):

        @pl.loop(1, PLANE)
        def _(d):
            x_copy(s, d, at_y(-dy)).wait_send()


def shards(
    fact_cells,
    gain_col,
    w_qkv,
    w_col_out,
    gain_tile,
    w_query,
    w_tile_out,
    tile_kv,
    tile_ids,
    key_mask,
    *,
    rows_n,
):
    maxt = tile_ids.shape[1]
    vmem = pl.BlockSpec(memory_space=pltpu.VMEM)
    smem = pl.BlockSpec(memory_space=pltpu.SMEM)
    anywhere = pl.BlockSpec(memory_space=pl.ANY)
    tiles = tile_kv.reshape(tile_kv.shape[0], tile_kv.shape[1], tile_kv.shape[3])
    dma = pltpu.SemaphoreType.DMA
    out = pl.pallas_call(
        functools.partial(layer_kernel, rows_n, maxt),
        out_shape=jax.ShapeDtypeStruct((ZN, GROUP, D), BF),
        in_specs=[smem, vmem, vmem, vmem, vmem, vmem] + [anywhere] * 4,
        out_specs=vmem,
        scratch_shapes=[
            pltpu.VMEM((ZN, GROUP, D), BF),
            pltpu.VMEM((CELLS, 3 * D), BF),
            pltpu.VMEM((ZN, GROUP, D), BF),
            pltpu.VMEM((ZN, GROUP, D), BF),
            pltpu.VMEM((ZN, CELLS // 2, 128), BF),
            pltpu.VMEM((ZN, CELLS // 2, 128), BF),
            pltpu.VMEM((ZN, ZN, GROUP, 128), BF),
            pltpu.VMEM((ZN, ZN, GROUP, 128), BF),
        ]
        + [pltpu.VMEM(tiles.shape, BF)] * 7
        + [
            pltpu.VMEM((8, PLANE, 128, 128), BF),
            pltpu.VMEM((rows_n, 128, 128), BF),
            pltpu.VMEM((maxt * 128, 128), BF),
            pltpu.VMEM((maxt * 128, 128), BF),
            pltpu.VMEM((8, 128), jnp.int32),
            pltpu.VMEM((PLANE, 8, 128), jnp.int32),
            pltpu.SMEM((PLANE, 8, 128), jnp.int32),
            pltpu.VMEM((D, 3 * D), BF),
            pltpu.VMEM((D, D), BF),
            pltpu.VMEM((D, D), BF),
            pltpu.VMEM((2 * D, D), BF),
            dma((3 + ZN,)),
            dma,
            dma((ZN,)),
            dma((ZN,)),
            dma((ZN,)),
            dma((ZN,)),
            dma((ZN,)),
            dma((ZN,)),
            dma((ZN,)),
            dma((ZN,)),
            dma((ZN, ZN)),
            dma((ZN, ZN)),
            dma((7,)),
            dma((7,)),
            dma((8, PLANE)),
            dma((8, PLANE)),
        ],
        compiler_params=pltpu.CompilerParams(
            collective_id=0, has_side_effects=True, vmem_limit_bytes=60 << 20
        ),
    )(
        tile_ids,
        key_mask,
        fact_cells.reshape(ZN, GROUP, D),
        gain_col.reshape(1, D),
        gain_tile.reshape(1, D),
        tiles,
        w_qkv,
        w_col_out,
        w_query,
        w_tile_out,
    )
    return out.reshape(fact_cells.shape)


def solution(mesh):
    placed = (
        P("rows", "cols", None),
        P(),
        P(),
        P(),
        P(),
        P(),
        P(),
        P("rows", None, "cols", None),
        P("rows", None),
        P("rows", None),
    )
    return jax.shard_map(
        functools.partial(shards, rows_n=mesh.shape["rows"]),
        mesh=mesh,
        in_specs=placed,
        out_specs=P("rows", "cols", None),
        check_vma=False,
    )
```

```python
import functools
import math

import jax
import jax.numpy as jnp
from jax import lax
from jax.experimental import pallas as pl
from jax.experimental.pallas import tpu as pltpu
from jax.sharding import PartitionSpec as P

F32, BF = jnp.float32, jnp.bfloat16
MESH = pl.DeviceIdType.MESH
NT = (((1,), (1,)), ((), ()))
ZN = 8
GROUP = 24
CELLS = ZN * GROUP
D = 512
EARLY_STEPS, EARLY = 6, 32
PARTS = ((0, 4), (4, 2))
LAST = 3
PLANE = 8
STEPS = ((0, 0), (1, 1), (-1, 5), (2, 2), (-2, 6), (3, 3), (-3, 7), (4, 4))


def rms(values, gain):
    mean_sq = jnp.mean(values * values, axis=-1, keepdims=True)
    return (values * lax.rsqrt(mean_sq + 1e-05) * gain).astype(BF)


def row_of(shape, dim, rows):
    return (lax.broadcasted_iota(jnp.int32, shape, dim) & (4 * rows - 1)) >> 2


def layer_kernel(
    rows_n,
    maxt,
    ids_ref,
    mask_hbm,
    fact_hbm,
    gain_col_hbm,
    gain_tile_hbm,
    tile_hbm,
    w_qkv_hbm,
    w_col_hbm,
    w_query_hbm,
    w_out_hbm,
    out_ref,
    mask_ref,
    fact_ref,
    gain_col_ref,
    gain_tile_ref,
    tile_ref,
    xin_a,
    xin_b,
    packed_a,
    packed_b,
    delta_send_a,
    delta_send_b,
    delta_buf_a,
    delta_buf_b,
    q_send_a,
    q_send_b,
    q_buf_a,
    q_buf_b,
    q_all,
    o_send_a,
    o_send_b,
    a_buf_a,
    a_buf_b,
    x_row,
    x_sib,
    y1,
    y2,
    y3,
    y4,
    y5,
    y6,
    y7,
    x_send,
    kv_early,
    kv_late,
    k_early,
    v_early,
    k_late,
    v_late,
    s_even,
    s_odd,
    o_first,
    m_first,
    o_even,
    my_list,
    lists,
    lists_s,
    w_qkv,
    w_col,
    w_query,
    w_twice,
    in_sem,
    w_sem,
    list_sem,
    y_sem,
    send_sem,
    recv_sem,
):
    row = lax.axis_index("rows")
    me = lax.axis_index("cols")
    seat = lax.rem(row, PLANE)
    base = row - seat

    def at_z(k):
        return lax.rem(me + k, ZN)

    def at_seat(d):
        return base + lax.rem(seat + d, PLANE)

    def at_y(dy):
        return lax.rem(row + dy * PLANE + rows_n, rows_n)

    def to_z(src, dst, ss, rs, k):
        return pltpu.make_async_remote_copy(
            src, dst, ss, rs, device_id=(row, at_z(k)), device_id_type=MESH
        )

    def to_row(src, dst, ss, rs, r):
        return pltpu.make_async_remote_copy(src, dst, ss, rs, device_id=(r, me), device_id_type=MESH)

    def whole_set(buf, count, ss, rs):
        part = buf.at[pl.ds(0, count)]
        return to_z(part, part, ss, rs, 1)

    def all_in(buf, count, n):
        whole_set(buf, count, send_sem.at[n], recv_sem.at[n]).wait_recv()

    def all_out(buf, count, n):
        whole_set(buf, count, send_sem.at[n], recv_sem.at[n]).wait_send()

    barrier = pltpu.get_barrier_semaphore()

    @pl.loop(1, ZN)
    def _(k):
        pl.semaphore_signal(barrier, inc=1, device_id=(row, at_z(k)), device_id_type=MESH)
        pl.semaphore_signal(barrier, inc=1, device_id=(at_seat(k), me), device_id_type=MESH)

    for dy in (1, -1):
        pl.semaphore_signal(barrier, inc=1, device_id=(at_y(dy), me), device_id_type=MESH)

    xin = (xin_a, xin_b)
    packed_buf = (packed_a, packed_b)
    delta_send = (delta_send_a, delta_send_b)
    delta_buf = (delta_buf_a, delta_buf_b)
    q_send = (q_send_a, q_send_b)
    q_buf = (q_buf_a, q_buf_b)
    o_send = (o_send_a, o_send_b)
    a_buf = (a_buf_a, a_buf_b)

    def cells_of(z, part):
        first, rows = PARTS[part]
        return fact_hbm.at[pl.ds(6 * z + first, rows)]

    tile_in = pltpu.make_async_copy(tile_hbm, tile_ref, in_sem.at[0])
    xin_in = [
        pltpu.make_async_copy(cells_of(me, part), xin[part].at[me], in_sem.at[6 * part + 1])
        for part in range(2)
    ]
    gain_in = pltpu.make_async_copy(gain_col_hbm, gain_col_ref, in_sem.at[2])
    gain2_in = pltpu.make_async_copy(gain_tile_hbm, gain_tile_ref, in_sem.at[3])
    mask_in = pltpu.make_async_copy(mask_hbm, mask_ref, in_sem.at[4])
    fact_in = pltpu.make_async_copy(fact_hbm, fact_ref, in_sem.at[5])
    w_copies = [
        pltpu.make_async_copy(w_qkv_hbm, w_qkv, w_sem.at[0]),
        pltpu.make_async_copy(w_col_hbm, w_col, w_sem.at[1]),
        pltpu.make_async_copy(w_query_hbm, w_query, w_sem.at[2]),
    ] + [
        pltpu.make_async_copy(
            w_out_hbm.at[pl.ds(64 * h, 64)], w_twice.at[pl.ds(64 * n, 64)], w_sem.at[3]
        )
        for n, h in enumerate(h for h in range(ZN) for _ in range(2))
    ]
    for copy in xin_in + [tile_in, gain_in, gain2_in, mask_in, fact_in] + w_copies:
        copy.start()

    lane8 = lax.broadcasted_iota(jnp.int32, (8, 128), 1)
    picks = jnp.zeros((8, 128), jnp.int32)
    order = jnp.zeros((8, 128), jnp.int32)
    y_me = row >> 3
    slots = []
    for j in range(maxt):
        slot_id = ids_ref[0, j]
        picks = jnp.where(lane8 == (slot_id >> 2), slot_id & 3, picks)
        owner = jnp.where(slot_id >= 0, slot_id >> 2, row)
        dy = (y_me - (owner >> 3)) & 7
        step = jnp.where(dy <= 4, jnp.maximum(2 * dy - 1, 0), 2 * (8 - dy))
        slots.append((step * 8 + (owner & 7), (step < EARLY_STEPS).astype(jnp.int32)))
    n_early = sum(early for _, early in slots)
    seen = jnp.int32(0)
    for j, (spot, early) in enumerate(slots):
        rank = jnp.where(early > 0, seen, n_early + (j - seen))
        order = jnp.where(lane8 == rank, spot * 64 + j, order)
        seen = seen + early
    my_list[...] = picks
    lists[0] = picks
    lists[PLANE] = order
    pl.semaphore_wait(barrier, 16)

    def cell_copy(k, part):
        return to_z(
            cells_of(at_z(k), part), xin[part].at[me], send_sem.at[part], recv_sem.at[part], k
        )

    def list_copy(k):
        return to_row(my_list, lists.at[k], send_sem.at[2], recv_sem.at[2], at_seat(k))

    for part in range(2):

        @pl.loop(1, ZN)
        def _(k):
            cell_copy(k, part).start()

    @pl.loop(1, PLANE)
    def _(k):
        list_copy(k).start()

    y_bufs = (None, y1, y2, y3, y4, y5, y6, y7)

    def y_forward(src, number, sign, half):
        part = pl.ds(2 * half, 2)
        to_row(
            src.at[part],
            y_bufs[number + 1].at[part],
            send_sem.at[4],
            y_sem.at[number, half],
            at_y(sign),
        ).start()

    for half in range(2):
        y_forward(tile_hbm, 0, 1, half)
        y_forward(tile_hbm, 4, -1, half)

    for k in range(1, 4):
        to_row(
            tile_hbm, x_row.at[k - 1], send_sem.at[3], recv_sem.at[3], at_seat(2 * k)
        ).start()

    def spot_of(s):
        if s < EARLY_STEPS:
            return kv_early.at[s * PLANE + seat]
        return kv_late.at[(s - EARLY_STEPS) * PLANE + seat]

    def x_copy(s, d):
        n = 5 if s < EARLY_STEPS else 6
        return to_row(
            x_send.at[s - 1, d - 1], spot_of(s), send_sem.at[n], recv_sem.at[n], at_seat(d)
        )

    def hand_out(s):
        dy, number = STEPS[s]
        src = y_bufs[number]
        owner = at_y(-dy)
        spot_of(s)[...] = src[lists_s[0, 0, owner]]

        @pl.loop(1, PLANE)
        def _(d):
            x_send[s - 1, d - 1] = src[lists_s[PLANE - d, 0, owner]]
            x_copy(s, d).start()

    def hand_out_row():
        core = row & 1
        for k in range(4):
            src = x_row.at[k - 1] if k else tile_ref
            owner = at_seat(PLANE - 2 * k)
            spot = kv_early.at[owner - base]
            spot[...] = src[lists_s[0, 0, owner]]
            x_sib[k] = src[lists_s[7 - 6 * core, 0, owner]]
            to_row(
                x_sib.at[k], spot, send_sem.at[5], recv_sem.at[5], row + 1 - 2 * core
            ).start()

    def relay(steps):
        for half in range(2):
            part = pl.ds(2 * half, 2)
            for s in steps:
                dy, number = STEPS[s]
                buf = y_bufs[number].at[part]
                sem = number - 1
                to_row(buf, buf, send_sem.at[4], y_sem.at[sem, half], at_y(1)).wait_recv()
                if 0 < dy < 4:
                    y_forward(y_bufs[number], number, 1, half)
                if -3 < dy < 0:
                    y_forward(y_bufs[number], number, -1, half)

    relay((1, 2))
    all_in(lists, PLANE - 1, 2)
    to_smem = pltpu.make_async_copy(lists, lists_s, list_sem)
    to_smem.start()
    to_smem.wait()
    hand_out(1)
    hand_out(2)

    def q_copy(k, part):
        return to_z(
            q_send[part].at[at_z(k)],
            q_buf[part].at[me],
            send_sem.at[8 + part],
            recv_sem.at[8 + part],
            k,
        )

    def delta_copy(k, part):
        return to_z(
            delta_send[part].at[at_z(k)],
            delta_buf[part].at[me],
            send_sem.at[10 + part],
            recv_sem.at[10 + part],
            k,
        )

    gain_in.wait()
    for part, (_, rows) in enumerate(PARTS):
        cells = ZN * 4 * rows
        all_in(xin[part], ZN - 1, part)
        xin_in[part].wait()
        x = xin[part][...].astype(F32).reshape(cells, D)
        normed = rms(x, gain_col_ref[...])
        if part == 0:
            w_copies[0].wait()
        packed = packed_buf[part]
        packed[...] = jnp.dot(normed, w_qkv[...], preferred_element_type=F32).astype(BF)

        same_row = row_of((cells, cells), 0, rows) == row_of((cells, cells), 1, rows)
        low = lax.broadcasted_iota(jnp.int32, (cells, 128), 1) < 64
        mixed = []
        for pair in range(4):
            q2 = packed[:, pl.ds(128 * pair, 128)]
            k2 = packed[:, pl.ds(D + 128 * pair, 128)]
            v2 = packed[:, pl.ds(2 * D + 128 * pair, 128)]
            outs = []
            for half in range(2):
                q1 = jnp.where(low if half == 0 else ~low, q2, jnp.zeros_like(q2))
                s = lax.dot_general(q1, k2, NT, preferred_element_type=F32) * 0.125
                s = jnp.where(same_row, s, -1e30)
                e = jnp.exp(s - jnp.max(s, axis=1, keepdims=True))
                w = (e / jnp.sum(e, axis=1, keepdims=True)).astype(BF)
                outs.append(jnp.dot(w, v2, preferred_element_type=F32))
            mixed.append(jnp.where(low, outs[0], outs[1]).astype(BF))
        mixed = jnp.concatenate(mixed, axis=1)
        if part == 0:
            w_copies[1].wait()
        delta = jnp.dot(mixed, w_col[...], preferred_element_type=F32)
        if part == 0:
            gain2_in.wait()
        normed2 = rms(x + delta, gain_tile_ref[...])
        if part == 0:
            w_copies[2].wait()
        asked = jnp.dot(normed2, w_query[...], preferred_element_type=F32)
        asked = asked * (0.125 * math.log2(math.e))
        lower = lax.broadcasted_iota(jnp.int32, (cells // 2, 128), 1) < 64
        for pair in range(4):
            top = asked[: cells // 2, 128 * pair : 128 * pair + 128]
            bot = asked[cells // 2 :, 128 * pair : 128 * pair + 128]
            q_send[part][2 * pair] = jnp.where(lower, top, pltpu.roll(bot, 64, 1)).astype(BF)
            q_send[part][2 * pair + 1] = jnp.where(lower, pltpu.roll(top, 64, 1), bot).astype(BF)
        delta_send[part][...] = delta.reshape(ZN, 4 * rows, D).astype(BF)
        q_buf[part][me] = q_send[part][me]
        delta_buf[part][me] = delta_send[part][me]

        @pl.loop(1, ZN)
        def _(k):
            q_copy(k, part).start()

        if part == 0:
            relay((3, 4))
            hand_out(3)
            hand_out(4)

    tile_in.wait()
    part_in = x_row.at[pl.ds(0, 3)]
    to_z(part_in, part_in, send_sem.at[3], recv_sem.at[3], 1).wait_recv()
    hand_out_row()

    @pl.loop(1, ZN)
    def _(k):
        for part in range(2):
            delta_copy(k, part).start()

    mask_in.wait()
    dead = jnp.where(mask_ref[...] > 0, 0.0, -1e30)
    rows_dev = dead.shape[0]
    dead = jnp.concatenate(
        [jnp.zeros((rows_dev, 64), F32), dead, jnp.zeros((rows_dev, 64 - maxt), F32)], axis=1
    ).astype(BF)
    relay((5, 6))
    hand_out(5)
    hand_out(6)

    @pl.loop(0, ZN)
    def _(z):
        at = 0
        for first, rows in PARTS:
            cells = ZN * 4 * rows
            mine = z * 6 + first + row_of((cells, rows_dev), 0, rows)
            pick = jnp.where(
                lax.broadcasted_iota(jnp.int32, (cells, rows_dev), 1) == mine, 1.0, 0.0
            )
            bias = jnp.dot(pick.astype(BF), dead, preferred_element_type=F32)
            q_all[z, at : at + cells] = bias.astype(BF)
            at += cells

    for part in range(2):
        all_in(q_buf[part], ZN - 1, 8 + part)

    @pl.loop(0, ZN)
    def _(z):
        at = 0
        for part, (_, rows) in enumerate(PARTS):
            half = ZN * 2 * rows
            q = q_buf[part][z].astype(F32)
            lower = lax.broadcasted_iota(jnp.int32, (half, 128), 1) < 64
            for queries in (q, pltpu.roll(q, 64, 1)):
                bias = q_all[z, at : at + half].astype(F32)
                q_all[z, at : at + half] = jnp.where(lower, queries, bias).astype(BF)
                at += half

    relay((7,))
    hand_out(7)

    lane = lax.broadcasted_iota(jnp.int32, (128, 128), 1)

    def place(n, kv, mark, k_ref, v_ref):
        kv = kv.astype(F32)
        at = pl.ds(pl.multiple_of(n * 128, 128), 128)
        k_ref[at, :] = jnp.where(lane < 64, kv, jnp.where(lane == 64 + mark, 1.0, 0.0)).astype(BF)
        v_ref[at, :] = jnp.where(lane < 64, jnp.where(lane == 0, 1.0, 0.0), kv).astype(BF)

    def sweep(k_ref, v_ref, width, finish, earlier):
        def stage(later, s_later, now, s_now, tops):
            found = None
            if later is not None:
                s = lax.dot_general(q_all[later], k_ref[...], NT, preferred_element_type=F32)
                s_later[:, :width] = s
                found = jnp.max(s, axis=1, keepdims=True)
                if earlier:
                    found = jnp.maximum(found, m_first[later, :, 0:1])
            if now is not None:
                p = jnp.exp2(s_now[:, :width] - tops).astype(BF)
                o = jnp.dot(p, v_ref[...], preferred_element_type=F32)
                finish(now, o, tops, s_now is s_odd)
            return found

        def two(i, tops):
            tops = stage(2 * i + 1, s_odd, 2 * i, s_even, tops)
            return stage(2 * i + 2, s_even, 2 * i + 1, s_odd, tops)

        tops = stage(0, s_even, None, None, None)
        tops = lax.fori_loop(0, ZN // 2 - 1, two, tops)
        tops = stage(ZN - 1, s_odd, ZN - 2, s_even, tops)
        stage(None, None, ZN - 1, s_odd, tops)

    all_in(kv_early, (EARLY_STEPS - 1) * (PLANE - 1) + 4, 5)
    @pl.loop(0, EARLY)
    def _(n):
        code = lists_s[PLANE, 0, n]
        spot = jnp.minimum(code >> 6, EARLY_STEPS * PLANE - 1)
        place(n, kv_early[spot], code & 63, k_early, v_early)

    def keep(z, o, tops, odd):
        o_first[z] = o
        m_first[z] = jnp.broadcast_to(tops, (CELLS, 128))

    sweep(k_early, v_early, EARLY * 128, keep, False)

    all_in(kv_late, (8 - EARLY_STEPS) * (PLANE - 1), 6)
    @pl.loop(EARLY, maxt)
    def _(n):
        code = lists_s[PLANE, 0, n]
        spot = code >> 6
        first = kv_early[jnp.minimum(spot, EARLY_STEPS * PLANE - 1)].astype(F32)
        second = kv_late[jnp.maximum(spot - EARLY_STEPS * PLANE, 0)].astype(F32)
        place(
            n - EARLY,
            jnp.where(spot < EARLY_STEPS * PLANE, first, second),
            code & 63,
            k_late,
            v_late,
        )

    def o_copy(pair, k, part):
        n = 12 + 2 * (pair >= LAST) + part
        return to_z(
            o_send[part].at[pair, at_z(k)],
            a_buf[part].at[pair, me],
            send_sem.at[12 + part],
            recv_sem.at[n],
            k,
        )

    def send(z, o, tops, odd):
        o = o + o_first[z] * jnp.exp2(m_first[z, :, 0:1] - tops)
        o = o / o[:, 0:1]
        if not odd:
            o_even[...] = pltpu.roll(o, 64, 1)
            return
        low = lax.broadcasted_iota(jnp.int32, (CELLS, 128), 1) < 64
        o = jnp.where(low, o_even[...], o)
        pair = z // 2 if isinstance(z, int) else z >> 1
        at = 0
        for part, (_, rows) in enumerate(PARTS):
            cells = ZN * 4 * rows
            o_send[part][pair] = o[at : at + cells].reshape(ZN, 4 * rows, 128).astype(BF)
            a_buf[part][pair, me] = o_send[part][pair, me]
            at += cells

        @pl.loop(1, ZN)
        def _(k):
            for part in range(2):
                o_copy(pair, k, part).start()

    sweep(k_late, v_late, (maxt - EARLY) * 128, send, True)

    pltpu.make_async_copy(w_twice, w_twice, w_sem.at[3]).wait()
    fact_in.wait()

    for part in range(2):
        all_in(delta_buf[part], ZN - 1, 10 + part)
    def joined(bufs):
        both = jnp.concatenate([buf.astype(F32) for buf in bufs], axis=1)
        return both.reshape(both.shape[0] * GROUP, both.shape[2])

    for first, last, n in ((0, LAST, 12), (LAST, ZN // 2, 14)):
        for part in range(2):
            came = a_buf[part].at[pl.ds(first, last - first), pl.ds(0, ZN - 1)]
            to_z(came, came, send_sem.at[12 + part], recv_sem.at[n + part], 1).wait_recv()
        pairs = last - first
        cells = pairs * GROUP
        low = lax.broadcasted_iota(jnp.int32, (cells, 128), 1) < 64
        heads = [joined([a_buf[part][first:last, h] for part in range(2)]) for h in range(ZN)]
        base_rows = fact_ref[12 * first : 12 * last].astype(F32).reshape(2 * cells, D)
        more = joined([delta_buf[part][2 * first : 2 * last] for part in range(2)])
        answer = jnp.concatenate(
            [
                jnp.concatenate([jnp.where(side, a, 0.0).astype(BF) for a in heads], axis=1)
                for side in (low, ~low)
            ],
            axis=0,
        )
        got = jnp.dot(answer, w_twice[...], preferred_element_type=F32)
        got = jnp.concatenate(
            [
                got[side * cells + GROUP * n : side * cells + GROUP * (n + 1)]
                for n in range(pairs)
                for side in range(2)
            ],
            axis=0,
        )
        final = base_rows + more + got
        out_ref[12 * first : 12 * last] = final.reshape(12 * pairs, 4, D).astype(BF)

    for part in range(2):
        all_out(xin[part], ZN - 1, part)
        all_out(q_send[part], ZN - 1, 8 + part)
        all_out(delta_send[part], ZN - 1, 10 + part)
        out = o_send[part].at[pl.ds(0, ZN // 2), pl.ds(0, ZN - 1)]
        to_z(out, out, send_sem.at[12 + part], recv_sem.at[12 + part], 1).wait_send()
    all_out(lists, PLANE - 1, 2)
    all_out(x_row, 3, 3)
    all_out(kv_early, 4 * 7, 4)
    all_out(kv_early, (EARLY_STEPS - 1) * (PLANE - 1) + 4, 5)
    all_out(kv_late, (8 - EARLY_STEPS) * (PLANE - 1), 6)


def shards(
    fact_cells,
    gain_col,
    w_qkv,
    w_col_out,
    gain_tile,
    w_query,
    w_tile_out,
    tile_kv,
    tile_ids,
    key_mask,
    *,
    rows_n,
):
    maxt = tile_ids.shape[1]
    vmem = pl.BlockSpec(memory_space=pltpu.VMEM)
    smem = pl.BlockSpec(memory_space=pltpu.SMEM)
    anywhere = pl.BlockSpec(memory_space=pl.ANY)
    tiles = tile_kv.reshape(tile_kv.shape[0], tile_kv.shape[1], tile_kv.shape[3])
    dma = pltpu.SemaphoreType.DMA
    return pl.pallas_call(
        functools.partial(layer_kernel, rows_n, maxt),
        out_shape=jax.ShapeDtypeStruct(fact_cells.shape, BF),
        in_specs=[smem] + [anywhere] * 9,
        out_specs=vmem,
        scratch_shapes=[
            pltpu.VMEM(key_mask.shape, jnp.int32),
            pltpu.VMEM(fact_cells.shape, BF),
            pltpu.VMEM((1, D), F32),
            pltpu.VMEM((1, D), F32),
            pltpu.VMEM(tiles.shape, BF),
            pltpu.VMEM((ZN, PARTS[0][1], 4, D), BF),
            pltpu.VMEM((ZN, PARTS[1][1], 4, D), BF),
            pltpu.VMEM((ZN * 4 * PARTS[0][1], 3 * D), BF),
            pltpu.VMEM((ZN * 4 * PARTS[1][1], 3 * D), BF),
        ]
        + [pltpu.VMEM((ZN, 4 * rows, D), BF) for _ in range(2) for _, rows in PARTS]
        + [pltpu.VMEM((ZN, ZN * 2 * rows, 128), BF) for _ in range(2) for _, rows in PARTS]
        + [pltpu.VMEM((ZN, CELLS, 128), BF)]
        + [pltpu.VMEM((ZN // 2, ZN, 4 * rows, 128), BF) for _ in range(2) for _, rows in PARTS]
        + [
            pltpu.VMEM((3,) + tiles.shape, BF),
            pltpu.VMEM((4, 128, 128), BF),
        ]
        + [pltpu.VMEM(tiles.shape, BF)] * 7
        + [
            pltpu.VMEM((7, PLANE - 1, 128, 128), BF),
            pltpu.VMEM((EARLY_STEPS * PLANE, 128, 128), BF),
            pltpu.VMEM(((8 - EARLY_STEPS) * PLANE, 128, 128), BF),
            pltpu.VMEM((EARLY * 128, 128), BF),
            pltpu.VMEM((EARLY * 128, 128), BF),
            pltpu.VMEM(((maxt - EARLY) * 128, 128), BF),
            pltpu.VMEM(((maxt - EARLY) * 128, 128), BF),
            pltpu.VMEM((CELLS, EARLY * 128), F32),
            pltpu.VMEM((CELLS, EARLY * 128), F32),
            pltpu.VMEM((ZN, CELLS, 128), F32),
            pltpu.VMEM((ZN, CELLS, 128), F32),
            pltpu.VMEM((CELLS, 128), F32),
            pltpu.VMEM((8, 128), jnp.int32),
            pltpu.VMEM((PLANE + 1, 8, 128), jnp.int32),
            pltpu.SMEM((PLANE + 1, 8, 128), jnp.int32),
            pltpu.VMEM((D, 3 * D), BF),
            pltpu.VMEM((D, D), BF),
            pltpu.VMEM((D, D), BF),
            pltpu.VMEM((2 * D, D), BF),
            dma((8,)),
            dma((4,)),
            dma,
            dma((7, 2)),
            dma((14,)),
            dma((16,)),
        ],
        compiler_params=pltpu.CompilerParams(
            collective_id=0, has_side_effects=True, vmem_limit_bytes=60 << 20
        ),
    )(
        tile_ids,
        key_mask,
        fact_cells,
        gain_col.reshape(1, D),
        gain_tile.reshape(1, D),
        tiles,
        w_qkv,
        w_col_out,
        w_query,
        w_tile_out,
    )


def solution(mesh):
    placed = (
        P("rows", "cols", None),
        P(),
        P(),
        P(),
        P(),
        P(),
        P(),
        P("rows", None, "cols", None),
        P("rows", None),
        P("rows", None),
    )
    return jax.shard_map(
        functools.partial(shards, rows_n=mesh.shape["rows"]),
        mesh=mesh,
        in_specs=placed,
        out_specs=P("rows", "cols", None),
        check_vma=False,
    )
```

```python
import functools
import math

import jax
import jax.numpy as jnp
from jax import lax
from jax.experimental import pallas as pl
from jax.experimental.pallas import tpu as pltpu
from jax.sharding import PartitionSpec as P

F32, BF = jnp.float32, jnp.bfloat16
MESH = pl.DeviceIdType.MESH
NT = (((1,), (1,)), ((), ()))
ZN = 8
GROUP = 24
CELLS = ZN * GROUP
D = 512
EARLY_STEPS, EARLY = 5, 24
PARTS = ((0, 4), (4, 2))
LAST = 3
PLANE = 8
STEPS = ((0, 0), (1, 1), (-1, 5), (2, 2), (-2, 6), (3, 3), (-3, 7), (4, 4))


def rms(values, gain):
    mean_sq = jnp.mean(values * values, axis=-1, keepdims=True)
    return (values * lax.rsqrt(mean_sq + 1e-05) * gain).astype(BF)


def row_of(shape, dim, rows):
    return (lax.broadcasted_iota(jnp.int32, shape, dim) & (4 * rows - 1)) >> 2


def layer_kernel(
    rows_n,
    maxt,
    ids_ref,
    mask_hbm,
    fact_hbm,
    gain_col_hbm,
    gain_tile_hbm,
    tile_hbm,
    w_qkv_hbm,
    w_col_hbm,
    w_query_hbm,
    w_out_hbm,
    out_ref,
    mask_ref,
    fact_ref,
    gain_col_ref,
    gain_tile_ref,
    tile_ref,
    xin_a,
    xin_b,
    packed_a,
    packed_b,
    delta_send_a,
    delta_send_b,
    delta_buf_a,
    delta_buf_b,
    q_send_a,
    q_send_b,
    q_buf_a,
    q_buf_b,
    q_all,
    o_send_a,
    o_send_b,
    a_buf_a,
    a_buf_b,
    x_row,
    x_sib,
    y1,
    y2,
    y3,
    y4,
    y5,
    y6,
    y7,
    x_send,
    kv_early,
    kv_late,
    k_early,
    v_early,
    k_late,
    v_late,
    s_even,
    s_odd,
    o_first,
    m_first,
    o_even,
    my_list,
    lists,
    lists_s,
    w_qkv,
    w_col,
    w_query,
    w_twice,
    in_sem,
    w_sem,
    list_sem,
    y_sem,
    send_sem,
    recv_sem,
):
    row = lax.axis_index("rows")
    me = lax.axis_index("cols")
    seat = lax.rem(row, PLANE)
    base = row - seat

    def at_z(k):
        return lax.rem(me + k, ZN)

    def at_seat(d):
        return base + lax.rem(seat + d, PLANE)

    def at_y(dy):
        return lax.rem(row + dy * PLANE + rows_n, rows_n)

    def to_z(src, dst, ss, rs, k):
        return pltpu.make_async_remote_copy(
            src, dst, ss, rs, device_id=(row, at_z(k)), device_id_type=MESH
        )

    def to_row(src, dst, ss, rs, r):
        return pltpu.make_async_remote_copy(src, dst, ss, rs, device_id=(r, me), device_id_type=MESH)

    def whole_set(buf, count, ss, rs):
        part = buf.at[pl.ds(0, count)]
        return to_z(part, part, ss, rs, 1)

    def all_in(buf, count, n):
        whole_set(buf, count, send_sem.at[n], recv_sem.at[n]).wait_recv()

    def all_out(buf, count, n):
        whole_set(buf, count, send_sem.at[n], recv_sem.at[n]).wait_send()

    barrier = pltpu.get_barrier_semaphore()

    @pl.loop(1, ZN)
    def _(k):
        pl.semaphore_signal(barrier, inc=1, device_id=(row, at_z(k)), device_id_type=MESH)
        pl.semaphore_signal(barrier, inc=1, device_id=(at_seat(k), me), device_id_type=MESH)

    for dy in (1, -1):
        pl.semaphore_signal(barrier, inc=1, device_id=(at_y(dy), me), device_id_type=MESH)

    xin = (xin_a, xin_b)
    packed_buf = (packed_a, packed_b)
    delta_send = (delta_send_a, delta_send_b)
    delta_buf = (delta_buf_a, delta_buf_b)
    q_send = (q_send_a, q_send_b)
    q_buf = (q_buf_a, q_buf_b)
    o_send = (o_send_a, o_send_b)
    a_buf = (a_buf_a, a_buf_b)

    def cells_of(z, part):
        first, rows = PARTS[part]
        return fact_hbm.at[pl.ds(6 * z + first, rows)]

    tile_in = pltpu.make_async_copy(tile_hbm, tile_ref, in_sem.at[0])
    xin_in = [
        pltpu.make_async_copy(cells_of(me, part), xin[part].at[me], in_sem.at[6 * part + 1])
        for part in range(2)
    ]
    gain_in = pltpu.make_async_copy(gain_col_hbm, gain_col_ref, in_sem.at[2])
    gain2_in = pltpu.make_async_copy(gain_tile_hbm, gain_tile_ref, in_sem.at[3])
    mask_in = pltpu.make_async_copy(mask_hbm, mask_ref, in_sem.at[4])
    fact_in = pltpu.make_async_copy(fact_hbm, fact_ref, in_sem.at[5])
    w_copies = [
        pltpu.make_async_copy(w_qkv_hbm, w_qkv, w_sem.at[0]),
        pltpu.make_async_copy(w_col_hbm, w_col, w_sem.at[1]),
        pltpu.make_async_copy(w_query_hbm, w_query, w_sem.at[2]),
    ] + [
        pltpu.make_async_copy(
            w_out_hbm.at[pl.ds(64 * h, 64)], w_twice.at[pl.ds(64 * n, 64)], w_sem.at[3]
        )
        for n, h in enumerate(h for h in range(ZN) for _ in range(2))
    ]
    for copy in xin_in + [tile_in, gain_in, gain2_in, mask_in, fact_in] + w_copies:
        copy.start()

    lane8 = lax.broadcasted_iota(jnp.int32, (8, 128), 1)
    picks = jnp.zeros((8, 128), jnp.int32)
    order = jnp.zeros((8, 128), jnp.int32)
    y_me = row >> 3
    slots = []
    for j in range(maxt):
        slot_id = ids_ref[0, j]
        picks = jnp.where(lane8 == (slot_id >> 2), slot_id & 3, picks)
        owner = jnp.where(slot_id >= 0, slot_id >> 2, row)
        dy = (y_me - (owner >> 3)) & 7
        step = jnp.where(dy <= 4, jnp.maximum(2 * dy - 1, 0), 2 * (8 - dy))
        slots.append((step * 8 + (owner & 7), (step < EARLY_STEPS).astype(jnp.int32)))
    n_early = sum(early for _, early in slots)
    seen = jnp.int32(0)
    for j, (spot, early) in enumerate(slots):
        rank = jnp.where(early > 0, seen, n_early + (j - seen))
        order = jnp.where(lane8 == rank, spot * 64 + j, order)
        seen = seen + early
    my_list[...] = picks
    lists[0] = picks
    lists[PLANE] = order
    pl.semaphore_wait(barrier, 16)

    def cell_copy(k, part):
        return to_z(
            cells_of(at_z(k), part), xin[part].at[me], send_sem.at[part], recv_sem.at[part], k
        )

    def list_copy(k):
        return to_row(my_list, lists.at[k], send_sem.at[2], recv_sem.at[2], at_seat(k))

    for part in range(2):

        @pl.loop(1, ZN)
        def _(k):
            cell_copy(k, part).start()

    @pl.loop(1, PLANE)
    def _(k):
        list_copy(k).start()

    y_bufs = (None, y1, y2, y3, y4, y5, y6, y7)

    def y_forward(src, number, sign, half):
        part = pl.ds(2 * half, 2)
        to_row(
            src.at[part],
            y_bufs[number + 1].at[part],
            send_sem.at[4],
            y_sem.at[number, half],
            at_y(sign),
        ).start()

    for half in range(2):
        y_forward(tile_hbm, 0, 1, half)
        y_forward(tile_hbm, 4, -1, half)

    for k in range(1, 4):
        to_row(
            tile_hbm, x_row.at[k - 1], send_sem.at[3], recv_sem.at[3], at_seat(2 * k)
        ).start()

    def spot_of(s):
        if s < EARLY_STEPS:
            return kv_early.at[s * PLANE + seat]
        return kv_late.at[(s - EARLY_STEPS) * PLANE + seat]

    def x_copy(s, d):
        n = 5 if s < EARLY_STEPS else 6
        return to_row(
            x_send.at[s - 1, d - 1], spot_of(s), send_sem.at[n], recv_sem.at[n], at_seat(d)
        )

    def hand_out(s):
        dy, number = STEPS[s]
        src = y_bufs[number]
        owner = at_y(-dy)
        spot_of(s)[...] = src[lists_s[0, 0, owner]]

        @pl.loop(1, PLANE)
        def _(d):
            x_send[s - 1, d - 1] = src[lists_s[PLANE - d, 0, owner]]
            x_copy(s, d).start()

    def hand_out_row():
        core = row & 1
        for k in range(4):
            src = x_row.at[k - 1] if k else tile_ref
            owner = at_seat(PLANE - 2 * k)
            spot = kv_early.at[owner - base]
            spot[...] = src[lists_s[0, 0, owner]]
            x_sib[k] = src[lists_s[7 - 6 * core, 0, owner]]
            to_row(
                x_sib.at[k], spot, send_sem.at[5], recv_sem.at[5], row + 1 - 2 * core
            ).start()

    def relay(steps):
        for half in range(2):
            part = pl.ds(2 * half, 2)
            for s in steps:
                dy, number = STEPS[s]
                buf = y_bufs[number].at[part]
                sem = number - 1
                to_row(buf, buf, send_sem.at[4], y_sem.at[sem, half], at_y(1)).wait_recv()
                if 0 < dy < 4:
                    y_forward(y_bufs[number], number, 1, half)
                if -3 < dy < 0:
                    y_forward(y_bufs[number], number, -1, half)

    all_in(lists, PLANE - 1, 2)
    to_smem = pltpu.make_async_copy(lists, lists_s, list_sem)
    to_smem.start()
    relay((1, 2))
    to_smem.wait()
    hand_out(1)
    hand_out(2)

    def q_copy(k, part):
        return to_z(
            q_send[part].at[at_z(k)],
            q_buf[part].at[me],
            send_sem.at[8 + part],
            recv_sem.at[8 + part],
            k,
        )

    def delta_copy(k, part):
        return to_z(
            delta_send[part].at[at_z(k)],
            delta_buf[part].at[me],
            send_sem.at[10 + part],
            recv_sem.at[10 + part],
            k,
        )

    gain_in.wait()
    for part, (_, rows) in enumerate(PARTS):
        cells = ZN * 4 * rows
        all_in(xin[part], ZN - 1, part)
        xin_in[part].wait()
        x = xin[part][...].astype(F32).reshape(cells, D)
        normed = rms(x, gain_col_ref[...])
        if part == 0:
            w_copies[0].wait()
        packed = packed_buf[part]
        packed[...] = jnp.dot(normed, w_qkv[...], preferred_element_type=F32).astype(BF)
        if part == 1:
            relay((3, 4))
            hand_out(3)
            hand_out(4)

        same_row = row_of((cells, cells), 0, rows) == row_of((cells, cells), 1, rows)
        low = lax.broadcasted_iota(jnp.int32, (cells, 128), 1) < 64
        mixed = []
        for pair in range(4):
            q2 = packed[:, pl.ds(128 * pair, 128)]
            k2 = packed[:, pl.ds(D + 128 * pair, 128)]
            v2 = packed[:, pl.ds(2 * D + 128 * pair, 128)]
            outs = []
            for half in range(2):
                q1 = jnp.where(low if half == 0 else ~low, q2, jnp.zeros_like(q2))
                s = lax.dot_general(q1, k2, NT, preferred_element_type=F32) * 0.125
                s = jnp.where(same_row, s, -1e30)
                e = jnp.exp(s - jnp.max(s, axis=1, keepdims=True))
                w = (e / jnp.sum(e, axis=1, keepdims=True)).astype(BF)
                outs.append(jnp.dot(w, v2, preferred_element_type=F32))
            mixed.append(jnp.where(low, outs[0], outs[1]).astype(BF))
        mixed = jnp.concatenate(mixed, axis=1)
        if part == 0:
            w_copies[1].wait()
        delta = jnp.dot(mixed, w_col[...], preferred_element_type=F32)
        if part == 0:
            gain2_in.wait()
        normed2 = rms(x + delta, gain_tile_ref[...])
        if part == 0:
            w_copies[2].wait()
        asked = jnp.dot(normed2, w_query[...], preferred_element_type=F32)
        asked = asked * (0.125 * math.log2(math.e))
        lower = lax.broadcasted_iota(jnp.int32, (cells // 2, 128), 1) < 64
        for pair in range(4):
            top = asked[: cells // 2, 128 * pair : 128 * pair + 128]
            bot = asked[cells // 2 :, 128 * pair : 128 * pair + 128]
            q_send[part][2 * pair] = jnp.where(lower, top, pltpu.roll(bot, 64, 1)).astype(BF)
            q_send[part][2 * pair + 1] = jnp.where(lower, pltpu.roll(top, 64, 1), bot).astype(BF)
        delta_send[part][...] = delta.reshape(ZN, 4 * rows, D).astype(BF)
        q_buf[part][me] = q_send[part][me]
        delta_buf[part][me] = delta_send[part][me]

        @pl.loop(1, ZN)
        def _(k):
            q_copy(k, part).start()

    tile_in.wait()
    part_in = x_row.at[pl.ds(0, 3)]
    to_z(part_in, part_in, send_sem.at[3], recv_sem.at[3], 1).wait_recv()
    hand_out_row()

    @pl.loop(1, ZN)
    def _(k):
        for part in range(2):
            delta_copy(k, part).start()

    mask_in.wait()
    dead = jnp.where(mask_ref[...] > 0, 0.0, -1e30)
    rows_dev = dead.shape[0]
    dead = jnp.concatenate(
        [jnp.zeros((rows_dev, 64), F32), dead, jnp.zeros((rows_dev, 64 - maxt), F32)], axis=1
    ).astype(BF)
    relay((5, 6))
    hand_out(5)
    hand_out(6)

    @pl.loop(0, ZN)
    def _(z):
        at = 0
        for first, rows in PARTS:
            cells = ZN * 4 * rows
            mine = z * 6 + first + row_of((cells, rows_dev), 0, rows)
            pick = jnp.where(
                lax.broadcasted_iota(jnp.int32, (cells, rows_dev), 1) == mine, 1.0, 0.0
            )
            bias = jnp.dot(pick.astype(BF), dead, preferred_element_type=F32)
            q_all[z, at : at + cells] = bias.astype(BF)
            at += cells

    for part in range(2):
        all_in(q_buf[part], ZN - 1, 8 + part)

    @pl.loop(0, ZN)
    def _(z):
        at = 0
        for part, (_, rows) in enumerate(PARTS):
            half = ZN * 2 * rows
            q = q_buf[part][z].astype(F32)
            lower = lax.broadcasted_iota(jnp.int32, (half, 128), 1) < 64
            for queries in (q, pltpu.roll(q, 64, 1)):
                bias = q_all[z, at : at + half].astype(F32)
                q_all[z, at : at + half] = jnp.where(lower, queries, bias).astype(BF)
                at += half

    relay((7,))
    hand_out(7)

    lane = lax.broadcasted_iota(jnp.int32, (128, 128), 1)

    def place(n, kv, mark, k_ref, v_ref):
        kv = kv.astype(F32)
        at = pl.ds(pl.multiple_of(n * 128, 128), 128)
        k_ref[at, :] = jnp.where(lane < 64, kv, jnp.where(lane == 64 + mark, 1.0, 0.0)).astype(BF)
        v_ref[at, :] = jnp.where(lane < 64, jnp.where(lane == 0, 1.0, 0.0), kv).astype(BF)

    def sweep(k_ref, v_ref, width, finish, earlier):
        def stage(later, s_later, now, s_now, tops):
            found = None
            if later is not None:
                s = lax.dot_general(q_all[later], k_ref[...], NT, preferred_element_type=F32)
                s_later[:, :width] = s
                found = jnp.max(s, axis=1, keepdims=True)
                if earlier:
                    found = jnp.maximum(found, m_first[later, :, 0:1])
            if now is not None:
                p = jnp.exp2(s_now[:, :width] - tops).astype(BF)
                o = jnp.dot(p, v_ref[...], preferred_element_type=F32)
                finish(now, o, tops, s_now is s_odd)
            return found

        def two(i, tops):
            tops = stage(2 * i + 1, s_odd, 2 * i, s_even, tops)
            return stage(2 * i + 2, s_even, 2 * i + 1, s_odd, tops)

        tops = stage(0, s_even, None, None, None)
        tops = lax.fori_loop(0, ZN // 2 - 1, two, tops)
        tops = stage(ZN - 1, s_odd, ZN - 2, s_even, tops)
        stage(None, None, ZN - 1, s_odd, tops)

    all_in(kv_early, (EARLY_STEPS - 1) * (PLANE - 1) + 4, 5)
    @pl.loop(0, EARLY)
    def _(n):
        code = lists_s[PLANE, 0, n]
        spot = jnp.minimum(code >> 6, EARLY_STEPS * PLANE - 1)
        place(n, kv_early[spot], code & 63, k_early, v_early)

    def keep(z, o, tops, odd):
        o_first[z] = o
        m_first[z] = jnp.broadcast_to(tops, (CELLS, 128))

    sweep(k_early, v_early, EARLY * 128, keep, False)

    all_in(kv_late, (8 - EARLY_STEPS) * (PLANE - 1), 6)
    @pl.loop(EARLY, maxt)
    def _(n):
        code = lists_s[PLANE, 0, n]
        spot = code >> 6
        first = kv_early[jnp.minimum(spot, EARLY_STEPS * PLANE - 1)].astype(F32)
        second = kv_late[jnp.maximum(spot - EARLY_STEPS * PLANE, 0)].astype(F32)
        place(
            n - EARLY,
            jnp.where(spot < EARLY_STEPS * PLANE, first, second),
            code & 63,
            k_late,
            v_late,
        )

    def o_copy(pair, k, part):
        n = 12 + 2 * (pair >= LAST) + part
        return to_z(
            o_send[part].at[pair, at_z(k)],
            a_buf[part].at[pair, me],
            send_sem.at[12 + part],
            recv_sem.at[n],
            k,
        )

    def send(z, o, tops, odd):
        o = o + o_first[z] * jnp.exp2(m_first[z, :, 0:1] - tops)
        o = o / o[:, 0:1]
        if not odd:
            o_even[...] = pltpu.roll(o, 64, 1)
            return
        low = lax.broadcasted_iota(jnp.int32, (CELLS, 128), 1) < 64
        o = jnp.where(low, o_even[...], o)
        pair = z // 2 if isinstance(z, int) else z >> 1
        at = 0
        for part, (_, rows) in enumerate(PARTS):
            cells = ZN * 4 * rows
            o_send[part][pair] = o[at : at + cells].reshape(ZN, 4 * rows, 128).astype(BF)
            a_buf[part][pair, me] = o_send[part][pair, me]
            at += cells

        @pl.loop(1, ZN)
        def _(k):
            for part in range(2):
                o_copy(pair, k, part).start()

    sweep(k_late, v_late, (maxt - EARLY) * 128, send, True)

    pltpu.make_async_copy(w_twice, w_twice, w_sem.at[3]).wait()
    fact_in.wait()

    for part in range(2):
        all_in(delta_buf[part], ZN - 1, 10 + part)
    def joined(bufs):
        both = jnp.concatenate([buf.astype(F32) for buf in bufs], axis=1)
        return both.reshape(both.shape[0] * GROUP, both.shape[2])

    for first, last, n in ((0, LAST, 12), (LAST, ZN // 2, 14)):
        for part in range(2):
            came = a_buf[part].at[pl.ds(first, last - first), pl.ds(0, ZN - 1)]
            to_z(came, came, send_sem.at[12 + part], recv_sem.at[n + part], 1).wait_recv()
        pairs = last - first
        cells = pairs * GROUP
        low = lax.broadcasted_iota(jnp.int32, (cells, 128), 1) < 64
        heads = [joined([a_buf[part][first:last, h] for part in range(2)]) for h in range(ZN)]
        base_rows = fact_ref[12 * first : 12 * last].astype(F32).reshape(2 * cells, D)
        more = joined([delta_buf[part][2 * first : 2 * last] for part in range(2)])
        answer = jnp.concatenate(
            [
                jnp.concatenate([jnp.where(side, a, 0.0).astype(BF) for a in heads], axis=1)
                for side in (low, ~low)
            ],
            axis=0,
        )
        got = jnp.dot(answer, w_twice[...], preferred_element_type=F32)
        got = jnp.concatenate(
            [
                got[side * cells + GROUP * n : side * cells + GROUP * (n + 1)]
                for n in range(pairs)
                for side in range(2)
            ],
            axis=0,
        )
        final = base_rows + more + got
        out_ref[12 * first : 12 * last] = final.reshape(12 * pairs, 4, D).astype(BF)

    for part in range(2):
        all_out(xin[part], ZN - 1, part)
        all_out(q_send[part], ZN - 1, 8 + part)
        all_out(delta_send[part], ZN - 1, 10 + part)
        out = o_send[part].at[pl.ds(0, ZN // 2), pl.ds(0, ZN - 1)]
        to_z(out, out, send_sem.at[12 + part], recv_sem.at[12 + part], 1).wait_send()
    all_out(lists, PLANE - 1, 2)
    all_out(x_row, 3, 3)
    all_out(kv_early, 4 * 7, 4)
    all_out(kv_early, (EARLY_STEPS - 1) * (PLANE - 1) + 4, 5)
    all_out(kv_late, (8 - EARLY_STEPS) * (PLANE - 1), 6)


def shards(
    fact_cells,
    gain_col,
    w_qkv,
    w_col_out,
    gain_tile,
    w_query,
    w_tile_out,
    tile_kv,
    tile_ids,
    key_mask,
    *,
    rows_n,
):
    maxt = tile_ids.shape[1]
    vmem = pl.BlockSpec(memory_space=pltpu.VMEM)
    smem = pl.BlockSpec(memory_space=pltpu.SMEM)
    anywhere = pl.BlockSpec(memory_space=pl.ANY)
    tiles = tile_kv.reshape(tile_kv.shape[0], tile_kv.shape[1], tile_kv.shape[3])
    dma = pltpu.SemaphoreType.DMA
    return pl.pallas_call(
        functools.partial(layer_kernel, rows_n, maxt),
        out_shape=jax.ShapeDtypeStruct(fact_cells.shape, BF),
        in_specs=[smem] + [anywhere] * 9,
        out_specs=vmem,
        scratch_shapes=[
            pltpu.VMEM(key_mask.shape, jnp.int32),
            pltpu.VMEM(fact_cells.shape, BF),
            pltpu.VMEM((1, D), F32),
            pltpu.VMEM((1, D), F32),
            pltpu.VMEM(tiles.shape, BF),
            pltpu.VMEM((ZN, PARTS[0][1], 4, D), BF),
            pltpu.VMEM((ZN, PARTS[1][1], 4, D), BF),
            pltpu.VMEM((ZN * 4 * PARTS[0][1], 3 * D), BF),
            pltpu.VMEM((ZN * 4 * PARTS[1][1], 3 * D), BF),
        ]
        + [pltpu.VMEM((ZN, 4 * rows, D), BF) for _ in range(2) for _, rows in PARTS]
        + [pltpu.VMEM((ZN, ZN * 2 * rows, 128), BF) for _ in range(2) for _, rows in PARTS]
        + [pltpu.VMEM((ZN, CELLS, 128), BF)]
        + [pltpu.VMEM((ZN // 2, ZN, 4 * rows, 128), BF) for _ in range(2) for _, rows in PARTS]
        + [
            pltpu.VMEM((3,) + tiles.shape, BF),
            pltpu.VMEM((4, 128, 128), BF),
        ]
        + [pltpu.VMEM(tiles.shape, BF)] * 7
        + [
            pltpu.VMEM((7, PLANE - 1, 128, 128), BF),
            pltpu.VMEM((EARLY_STEPS * PLANE, 128, 128), BF),
            pltpu.VMEM(((8 - EARLY_STEPS) * PLANE, 128, 128), BF),
            pltpu.VMEM((EARLY * 128, 128), BF),
            pltpu.VMEM((EARLY * 128, 128), BF),
            pltpu.VMEM(((maxt - EARLY) * 128, 128), BF),
            pltpu.VMEM(((maxt - EARLY) * 128, 128), BF),
            pltpu.VMEM((CELLS, EARLY * 128), F32),
            pltpu.VMEM((CELLS, EARLY * 128), F32),
            pltpu.VMEM((ZN, CELLS, 128), F32),
            pltpu.VMEM((ZN, CELLS, 128), F32),
            pltpu.VMEM((CELLS, 128), F32),
            pltpu.VMEM((8, 128), jnp.int32),
            pltpu.VMEM((PLANE + 1, 8, 128), jnp.int32),
            pltpu.SMEM((PLANE + 1, 8, 128), jnp.int32),
            pltpu.VMEM((D, 3 * D), BF),
            pltpu.VMEM((D, D), BF),
            pltpu.VMEM((D, D), BF),
            pltpu.VMEM((2 * D, D), BF),
            dma((8,)),
            dma((4,)),
            dma,
            dma((7, 2)),
            dma((14,)),
            dma((16,)),
        ],
        compiler_params=pltpu.CompilerParams(
            collective_id=0, has_side_effects=True, vmem_limit_bytes=60 << 20
        ),
    )(
        tile_ids,
        key_mask,
        fact_cells,
        gain_col.reshape(1, D),
        gain_tile.reshape(1, D),
        tiles,
        w_qkv,
        w_col_out,
        w_query,
        w_tile_out,
    )


def solution(mesh):
    placed = (
        P("rows", "cols", None),
        P(),
        P(),
        P(),
        P(),
        P(),
        P(),
        P("rows", None, "cols", None),
        P("rows", None),
        P("rows", None),
    )
    return jax.shard_map(
        functools.partial(shards, rows_n=mesh.shape["rows"]),
        mesh=mesh,
        in_specs=placed,
        out_specs=P("rows", "cols", None),
        check_vma=False,
    )
```

```python
import functools
import math

import jax
import jax.numpy as jnp
from jax import lax
from jax.experimental import pallas as pl
from jax.experimental.pallas import tpu as pltpu
from jax.sharding import PartitionSpec as P

F32, BF = jnp.float32, jnp.bfloat16
MESH = pl.DeviceIdType.MESH
NT = (((1,), (1,)), ((), ()))
ZN = 8
GROUP = 24
CELLS = ZN * GROUP
D = 512
EARLY_STEPS, EARLY = 5, 24
PARTS = ((0, 4), (4, 2))
LAST = 3
PLANE = 8
STEPS = ((0, 0), (1, 1), (-1, 5), (2, 2), (-2, 6), (3, 3), (-3, 7), (4, 4))


def rms(values, gain):
    mean_sq = jnp.mean(values * values, axis=-1, keepdims=True)
    return (values * lax.rsqrt(mean_sq + 1e-05) * gain).astype(BF)


def row_of(shape, dim, rows):
    return (lax.broadcasted_iota(jnp.int32, shape, dim) & (4 * rows - 1)) >> 2


def layer_kernel(
    rows_n,
    maxt,
    ids_ref,
    mask_hbm,
    fact_hbm,
    gain_col_hbm,
    gain_tile_hbm,
    tile_hbm,
    w_qkv_hbm,
    w_col_hbm,
    w_query_hbm,
    w_out_hbm,
    out_ref,
    mask_ref,
    fact_ref,
    gain_col_ref,
    gain_tile_ref,
    tile_ref,
    xin_a,
    xin_b,
    packed_a,
    packed_b,
    delta_send_a,
    delta_send_b,
    delta_buf_a,
    delta_buf_b,
    q_send_a,
    q_send_b,
    q_buf_a,
    q_buf_b,
    q_all,
    o_send_a,
    o_send_b,
    a_buf_a,
    a_buf_b,
    x_row,
    x_sib,
    y1,
    y2,
    y3,
    y4,
    y5,
    y6,
    y7,
    x_send,
    kv_early,
    kv_late,
    k_early,
    v_early,
    k_late,
    v_late,
    s_even,
    s_odd,
    o_first,
    m_first,
    o_even,
    my_list,
    lists,
    lists_s,
    w_qkv,
    w_col,
    w_query,
    w_twice,
    in_sem,
    w_sem,
    list_sem,
    y_sem,
    send_sem,
    recv_sem,
):
    row = lax.axis_index("rows")
    me = lax.axis_index("cols")
    seat = lax.rem(row, PLANE)
    base = row - seat

    def at_z(k):
        return lax.rem(me + k, ZN)

    def at_seat(d):
        return base + lax.rem(seat + d, PLANE)

    def at_y(dy):
        return lax.rem(row + dy * PLANE + rows_n, rows_n)

    def to_z(src, dst, ss, rs, k):
        return pltpu.make_async_remote_copy(
            src, dst, ss, rs, device_id=(row, at_z(k)), device_id_type=MESH
        )

    def to_row(src, dst, ss, rs, r):
        return pltpu.make_async_remote_copy(src, dst, ss, rs, device_id=(r, me), device_id_type=MESH)

    def whole_set(buf, count, ss, rs):
        part = buf.at[pl.ds(0, count)]
        return to_z(part, part, ss, rs, 1)

    def all_in(buf, count, n):
        whole_set(buf, count, send_sem.at[n], recv_sem.at[n]).wait_recv()

    def all_out(buf, count, n):
        whole_set(buf, count, send_sem.at[n], recv_sem.at[n]).wait_send()

    barrier = pltpu.get_barrier_semaphore()

    @pl.loop(1, ZN)
    def _(k):
        pl.semaphore_signal(barrier, inc=1, device_id=(row, at_z(k)), device_id_type=MESH)
        pl.semaphore_signal(barrier, inc=1, device_id=(at_seat(k), me), device_id_type=MESH)

    for dy in (1, -1):
        pl.semaphore_signal(barrier, inc=1, device_id=(at_y(dy), me), device_id_type=MESH)

    xin = (xin_a, xin_b)
    packed_buf = (packed_a, packed_b)
    delta_send = (delta_send_a, delta_send_b)
    delta_buf = (delta_buf_a, delta_buf_b)
    q_send = (q_send_a, q_send_b)
    q_buf = (q_buf_a, q_buf_b)
    o_send = (o_send_a, o_send_b)
    a_buf = (a_buf_a, a_buf_b)

    def cells_of(z, part):
        first, rows = PARTS[part]
        return fact_hbm.at[pl.ds(6 * z + first, rows)]

    tile_in = pltpu.make_async_copy(tile_hbm, tile_ref, in_sem.at[0])
    xin_in = [
        pltpu.make_async_copy(cells_of(me, part), xin[part].at[me], in_sem.at[6 * part + 1])
        for part in range(2)
    ]
    gain_in = pltpu.make_async_copy(gain_col_hbm, gain_col_ref, in_sem.at[2])
    gain2_in = pltpu.make_async_copy(gain_tile_hbm, gain_tile_ref, in_sem.at[3])
    mask_in = pltpu.make_async_copy(mask_hbm, mask_ref, in_sem.at[4])
    fact_in = pltpu.make_async_copy(fact_hbm, fact_ref, in_sem.at[5])
    w_copies = [
        pltpu.make_async_copy(w_qkv_hbm, w_qkv, w_sem.at[0]),
        pltpu.make_async_copy(w_col_hbm, w_col, w_sem.at[1]),
        pltpu.make_async_copy(w_query_hbm, w_query, w_sem.at[2]),
    ] + [
        pltpu.make_async_copy(
            w_out_hbm.at[pl.ds(64 * h, 64)], w_twice.at[pl.ds(64 * n, 64)], w_sem.at[3]
        )
        for n, h in enumerate(h for h in range(ZN) for _ in range(2))
    ]
    for copy in xin_in + [tile_in, gain_in, gain2_in, mask_in, fact_in] + w_copies:
        copy.start()

    lane8 = lax.broadcasted_iota(jnp.int32, (8, 128), 1)
    picks = jnp.zeros((8, 128), jnp.int32)
    order = jnp.zeros((8, 128), jnp.int32)
    y_me = row >> 3
    slots = []
    for j in range(maxt):
        slot_id = ids_ref[0, j]
        picks = jnp.where(lane8 == (slot_id >> 2), slot_id & 3, picks)
        owner = jnp.where(slot_id >= 0, slot_id >> 2, row)
        dy = (y_me - (owner >> 3)) & 7
        step = jnp.where(dy <= 4, jnp.maximum(2 * dy - 1, 0), 2 * (8 - dy))
        slots.append((step * 8 + (owner & 7), (step < EARLY_STEPS).astype(jnp.int32)))
    n_early = sum(early for _, early in slots)
    seen = jnp.int32(0)
    for j, (spot, early) in enumerate(slots):
        rank = jnp.where(early > 0, seen, n_early + (j - seen))
        order = jnp.where(lane8 == rank, spot * 64 + j, order)
        seen = seen + early
    my_list[...] = picks
    lists[0] = picks
    lists[PLANE] = order
    pl.semaphore_wait(barrier, 16)

    def cell_copy(k, part):
        return to_z(
            cells_of(at_z(k), part), xin[part].at[me], send_sem.at[part], recv_sem.at[part], k
        )

    def list_copy(k):
        return to_row(my_list, lists.at[k], send_sem.at[2], recv_sem.at[2], at_seat(k))

    for part in range(2):

        @pl.loop(1, ZN)
        def _(k):
            cell_copy(k, part).start()

    @pl.loop(1, PLANE)
    def _(k):
        list_copy(k).start()

    y_bufs = (None, y1, y2, y3, y4, y5, y6, y7)

    def y_forward(src, number, sign, half):
        part = pl.ds(2 * half, 2)
        to_row(
            src.at[part],
            y_bufs[number + 1].at[part],
            send_sem.at[4],
            y_sem.at[number, half],
            at_y(sign),
        ).start()

    for half in range(2):
        y_forward(tile_hbm, 0, 1, half)
        y_forward(tile_hbm, 4, -1, half)

    for k in range(1, 4):
        to_row(
            tile_hbm, x_row.at[k - 1], send_sem.at[3], recv_sem.at[3], at_seat(2 * k)
        ).start()

    def spot_of(s):
        if s < EARLY_STEPS:
            return kv_early.at[s * PLANE + seat]
        return kv_late.at[(s - EARLY_STEPS) * PLANE + seat]

    def x_copy(s, d):
        n = 5 if s < EARLY_STEPS else 6
        return to_row(
            x_send.at[s - 1, d - 1], spot_of(s), send_sem.at[n], recv_sem.at[n], at_seat(d)
        )

    def hand_out(s):
        dy, number = STEPS[s]
        src = y_bufs[number]
        owner = at_y(-dy)
        spot_of(s)[...] = src[lists_s[0, 0, owner]]

        @pl.loop(1, PLANE)
        def _(d):
            x_send[s - 1, d - 1] = src[lists_s[PLANE - d, 0, owner]]
            x_copy(s, d).start()

    def hand_out_row():
        core = row & 1
        for k in range(4):
            src = x_row.at[k - 1] if k else tile_ref
            owner = at_seat(PLANE - 2 * k)
            spot = kv_early.at[owner - base]
            spot[...] = src[lists_s[0, 0, owner]]
            x_sib[k] = src[lists_s[7 - 6 * core, 0, owner]]
            to_row(
                x_sib.at[k], spot, send_sem.at[5], recv_sem.at[5], row + 1 - 2 * core
            ).start()

    def relay(steps):
        for half in range(2):
            part = pl.ds(2 * half, 2)
            for s in steps:
                dy, number = STEPS[s]
                buf = y_bufs[number].at[part]
                sem = number - 1
                to_row(buf, buf, send_sem.at[4], y_sem.at[sem, half], at_y(1)).wait_recv()
                if 0 < dy < 4:
                    y_forward(y_bufs[number], number, 1, half)
                if -3 < dy < 0:
                    y_forward(y_bufs[number], number, -1, half)

    all_in(lists, PLANE - 1, 2)
    to_smem = pltpu.make_async_copy(lists, lists_s, list_sem)
    to_smem.start()
    relay((1, 2))
    to_smem.wait()
    hand_out(1)
    hand_out(2)

    def q_copy(k, part):
        return to_z(
            q_send[part].at[at_z(k)],
            q_buf[part].at[me],
            send_sem.at[8 + part],
            recv_sem.at[8 + part],
            k,
        )

    def delta_copy(k, part):
        return to_z(
            delta_send[part].at[at_z(k)],
            delta_buf[part].at[me],
            send_sem.at[10 + part],
            recv_sem.at[10 + part],
            k,
        )

    gain_in.wait()
    for part, (_, rows) in enumerate(PARTS):
        cells = ZN * 4 * rows
        all_in(xin[part], ZN - 1, part)
        xin_in[part].wait()
        x = xin[part][...].astype(F32).reshape(cells, D)
        normed = rms(x, gain_col_ref[...])
        if part == 0:
            w_copies[0].wait()
        packed = packed_buf[part]
        packed[...] = jnp.dot(normed, w_qkv[...], preferred_element_type=F32).astype(BF)
        if part == 1:
            relay((3, 4))
            hand_out(3)
            hand_out(4)

        same_row = row_of((cells, cells), 0, rows) == row_of((cells, cells), 1, rows)
        low = lax.broadcasted_iota(jnp.int32, (cells, 128), 1) < 64
        mixed = []
        for pair in range(4):
            q2 = packed[:, pl.ds(128 * pair, 128)]
            k2 = packed[:, pl.ds(D + 128 * pair, 128)]
            v2 = packed[:, pl.ds(2 * D + 128 * pair, 128)]
            outs = []
            for half in range(2):
                q1 = jnp.where(low if half == 0 else ~low, q2, jnp.zeros_like(q2))
                s = lax.dot_general(q1, k2, NT, preferred_element_type=F32) * 0.125
                s = jnp.where(same_row, s, -1e30)
                e = jnp.exp(s - jnp.max(s, axis=1, keepdims=True))
                w = (e / jnp.sum(e, axis=1, keepdims=True)).astype(BF)
                outs.append(jnp.dot(w, v2, preferred_element_type=F32))
            mixed.append(jnp.where(low, outs[0], outs[1]).astype(BF))
        mixed = jnp.concatenate(mixed, axis=1)
        if part == 0:
            w_copies[1].wait()
        delta = jnp.dot(mixed, w_col[...], preferred_element_type=F32)
        if part == 0:
            gain2_in.wait()
        normed2 = rms(x + delta, gain_tile_ref[...])
        if part == 0:
            w_copies[2].wait()
        asked = jnp.dot(normed2, w_query[...], preferred_element_type=F32)
        asked = asked * (0.125 * math.log2(math.e))
        lower = lax.broadcasted_iota(jnp.int32, (cells // 2, 128), 1) < 64
        for pair in range(4):
            top = asked[: cells // 2, 128 * pair : 128 * pair + 128]
            bot = asked[cells // 2 :, 128 * pair : 128 * pair + 128]
            q_send[part][2 * pair] = jnp.where(lower, top, pltpu.roll(bot, 64, 1)).astype(BF)
            q_send[part][2 * pair + 1] = jnp.where(lower, pltpu.roll(top, 64, 1), bot).astype(BF)
        delta_send[part][...] = delta.reshape(ZN, 4 * rows, D).astype(BF)
        q_buf[part][me] = q_send[part][me]
        delta_buf[part][me] = delta_send[part][me]

        @pl.loop(1, ZN)
        def _(k):
            q_copy(k, part).start()

    tile_in.wait()
    part_in = x_row.at[pl.ds(0, 3)]
    to_z(part_in, part_in, send_sem.at[3], recv_sem.at[3], 1).wait_recv()
    hand_out_row()

    mask_in.wait()
    dead = jnp.where(mask_ref[...] > 0, 0.0, -1e30)
    rows_dev = dead.shape[0]
    dead = jnp.concatenate(
        [jnp.zeros((rows_dev, 64), F32), dead, jnp.zeros((rows_dev, 64 - maxt), F32)], axis=1
    ).astype(BF)
    relay((5, 6))
    hand_out(5)
    hand_out(6)

    @pl.loop(0, ZN)
    def _(z):
        at = 0
        for first, rows in PARTS:
            cells = ZN * 4 * rows
            mine = z * 6 + first + row_of((cells, rows_dev), 0, rows)
            pick = jnp.where(
                lax.broadcasted_iota(jnp.int32, (cells, rows_dev), 1) == mine, 1.0, 0.0
            )
            bias = jnp.dot(pick.astype(BF), dead, preferred_element_type=F32)
            q_all[z, at : at + cells] = bias.astype(BF)
            at += cells

    lane = lax.broadcasted_iota(jnp.int32, (128, 128), 1)

    def place(n, kv, mark, k_ref, v_ref):
        kv = kv.astype(F32)
        at = pl.ds(pl.multiple_of(n * 128, 128), 128)
        k_ref[at, :] = jnp.where(lane < 64, kv, jnp.where(lane == 64 + mark, 1.0, 0.0)).astype(BF)
        v_ref[at, :] = jnp.where(lane < 64, jnp.where(lane == 0, 1.0, 0.0), kv).astype(BF)

    all_in(kv_early, (EARLY_STEPS - 1) * (PLANE - 1) + 4, 5)
    @pl.loop(0, EARLY)
    def _(n):
        code = lists_s[PLANE, 0, n]
        spot = jnp.minimum(code >> 6, EARLY_STEPS * PLANE - 1)
        place(n, kv_early[spot], code & 63, k_early, v_early)

    relay((7,))
    hand_out(7)

    for part in range(2):
        all_in(q_buf[part], ZN - 1, 8 + part)

    @pl.loop(1, ZN)
    def _(k):
        for part in range(2):
            delta_copy(k, part).start()

    @pl.loop(0, ZN)
    def _(z):
        at = 0
        for part, (_, rows) in enumerate(PARTS):
            half = ZN * 2 * rows
            q = q_buf[part][z].astype(F32)
            lower = lax.broadcasted_iota(jnp.int32, (half, 128), 1) < 64
            for queries in (q, pltpu.roll(q, 64, 1)):
                bias = q_all[z, at : at + half].astype(F32)
                q_all[z, at : at + half] = jnp.where(lower, queries, bias).astype(BF)
                at += half

    def sweep(k_ref, v_ref, width, finish, earlier):
        def stage(later, s_later, now, s_now, tops):
            found = None
            if later is not None:
                s = lax.dot_general(q_all[later], k_ref[...], NT, preferred_element_type=F32)
                s_later[:, :width] = s
                found = jnp.max(s, axis=1, keepdims=True)
                if earlier:
                    found = jnp.maximum(found, m_first[later, :, 0:1])
            if now is not None:
                p = jnp.exp2(s_now[:, :width] - tops).astype(BF)
                o = jnp.dot(p, v_ref[...], preferred_element_type=F32)
                finish(now, o, tops, s_now is s_odd)
            return found

        def two(i, tops):
            tops = stage(2 * i + 1, s_odd, 2 * i, s_even, tops)
            return stage(2 * i + 2, s_even, 2 * i + 1, s_odd, tops)

        tops = stage(0, s_even, None, None, None)
        tops = lax.fori_loop(0, ZN // 2 - 1, two, tops)
        tops = stage(ZN - 1, s_odd, ZN - 2, s_even, tops)
        stage(None, None, ZN - 1, s_odd, tops)

    def keep(z, o, tops, odd):
        o_first[z] = o
        m_first[z] = jnp.broadcast_to(tops, (CELLS, 128))

    sweep(k_early, v_early, EARLY * 128, keep, False)

    all_in(kv_late, (8 - EARLY_STEPS) * (PLANE - 1), 6)
    @pl.loop(EARLY, maxt)
    def _(n):
        code = lists_s[PLANE, 0, n]
        spot = code >> 6
        first = kv_early[jnp.minimum(spot, EARLY_STEPS * PLANE - 1)].astype(F32)
        second = kv_late[jnp.maximum(spot - EARLY_STEPS * PLANE, 0)].astype(F32)
        place(
            n - EARLY,
            jnp.where(spot < EARLY_STEPS * PLANE, first, second),
            code & 63,
            k_late,
            v_late,
        )

    def o_copy(pair, k, part):
        n = 12 + 2 * (pair >= LAST) + part
        return to_z(
            o_send[part].at[pair, at_z(k)],
            a_buf[part].at[pair, me],
            send_sem.at[12 + part],
            recv_sem.at[n],
            k,
        )

    def send(z, o, tops, odd):
        o = o + o_first[z] * jnp.exp2(m_first[z, :, 0:1] - tops)
        o = o / o[:, 0:1]
        if not odd:
            o_even[...] = pltpu.roll(o, 64, 1)
            return
        low = lax.broadcasted_iota(jnp.int32, (CELLS, 128), 1) < 64
        o = jnp.where(low, o_even[...], o)
        pair = z // 2 if isinstance(z, int) else z >> 1
        at = 0
        for part, (_, rows) in enumerate(PARTS):
            cells = ZN * 4 * rows
            o_send[part][pair] = o[at : at + cells].reshape(ZN, 4 * rows, 128).astype(BF)
            a_buf[part][pair, me] = o_send[part][pair, me]
            at += cells

        @pl.loop(1, ZN)
        def _(k):
            for part in range(2):
                o_copy(pair, k, part).start()

    sweep(k_late, v_late, (maxt - EARLY) * 128, send, True)

    pltpu.make_async_copy(w_twice, w_twice, w_sem.at[3]).wait()
    fact_in.wait()

    for part in range(2):
        all_in(delta_buf[part], ZN - 1, 10 + part)
    def joined(bufs):
        both = jnp.concatenate([buf.astype(F32) for buf in bufs], axis=1)
        return both.reshape(both.shape[0] * GROUP, both.shape[2])

    for first, last, n in ((0, LAST, 12), (LAST, ZN // 2, 14)):
        for part in range(2):
            came = a_buf[part].at[pl.ds(first, last - first), pl.ds(0, ZN - 1)]
            to_z(came, came, send_sem.at[12 + part], recv_sem.at[n + part], 1).wait_recv()
        pairs = last - first
        cells = pairs * GROUP
        low = lax.broadcasted_iota(jnp.int32, (cells, 128), 1) < 64
        heads = [joined([a_buf[part][first:last, h] for part in range(2)]) for h in range(ZN)]
        base_rows = fact_ref[12 * first : 12 * last].astype(F32).reshape(2 * cells, D)
        more = joined([delta_buf[part][2 * first : 2 * last] for part in range(2)])
        answer = jnp.concatenate(
            [
                jnp.concatenate([jnp.where(side, a, 0.0).astype(BF) for a in heads], axis=1)
                for side in (low, ~low)
            ],
            axis=0,
        )
        got = jnp.dot(answer, w_twice[...], preferred_element_type=F32)
        got = jnp.concatenate(
            [
                got[side * cells + GROUP * n : side * cells + GROUP * (n + 1)]
                for n in range(pairs)
                for side in range(2)
            ],
            axis=0,
        )
        final = base_rows + more + got
        out_ref[12 * first : 12 * last] = final.reshape(12 * pairs, 4, D).astype(BF)

    for part in range(2):
        all_out(xin[part], ZN - 1, part)
        all_out(q_send[part], ZN - 1, 8 + part)
        all_out(delta_send[part], ZN - 1, 10 + part)
        out = o_send[part].at[pl.ds(0, ZN // 2), pl.ds(0, ZN - 1)]
        to_z(out, out, send_sem.at[12 + part], recv_sem.at[12 + part], 1).wait_send()
    all_out(lists, PLANE - 1, 2)
    all_out(x_row, 3, 3)
    all_out(kv_early, 4 * 7, 4)
    all_out(kv_early, (EARLY_STEPS - 1) * (PLANE - 1) + 4, 5)
    all_out(kv_late, (8 - EARLY_STEPS) * (PLANE - 1), 6)


def shards(
    fact_cells,
    gain_col,
    w_qkv,
    w_col_out,
    gain_tile,
    w_query,
    w_tile_out,
    tile_kv,
    tile_ids,
    key_mask,
    *,
    rows_n,
):
    maxt = tile_ids.shape[1]
    vmem = pl.BlockSpec(memory_space=pltpu.VMEM)
    smem = pl.BlockSpec(memory_space=pltpu.SMEM)
    anywhere = pl.BlockSpec(memory_space=pl.ANY)
    tiles = tile_kv.reshape(tile_kv.shape[0], tile_kv.shape[1], tile_kv.shape[3])
    dma = pltpu.SemaphoreType.DMA
    return pl.pallas_call(
        functools.partial(layer_kernel, rows_n, maxt),
        out_shape=jax.ShapeDtypeStruct(fact_cells.shape, BF),
        in_specs=[smem] + [anywhere] * 9,
        out_specs=vmem,
        scratch_shapes=[
            pltpu.VMEM(key_mask.shape, jnp.int32),
            pltpu.VMEM(fact_cells.shape, BF),
            pltpu.VMEM((1, D), F32),
            pltpu.VMEM((1, D), F32),
            pltpu.VMEM(tiles.shape, BF),
            pltpu.VMEM((ZN, PARTS[0][1], 4, D), BF),
            pltpu.VMEM((ZN, PARTS[1][1], 4, D), BF),
            pltpu.VMEM((ZN * 4 * PARTS[0][1], 3 * D), BF),
            pltpu.VMEM((ZN * 4 * PARTS[1][1], 3 * D), BF),
        ]
        + [pltpu.VMEM((ZN, 4 * rows, D), BF) for _ in range(2) for _, rows in PARTS]
        + [pltpu.VMEM((ZN, ZN * 2 * rows, 128), BF) for _ in range(2) for _, rows in PARTS]
        + [pltpu.VMEM((ZN, CELLS, 128), BF)]
        + [pltpu.VMEM((ZN // 2, ZN, 4 * rows, 128), BF) for _ in range(2) for _, rows in PARTS]
        + [
            pltpu.VMEM((3,) + tiles.shape, BF),
            pltpu.VMEM((4, 128, 128), BF),
        ]
        + [pltpu.VMEM(tiles.shape, BF)] * 7
        + [
            pltpu.VMEM((7, PLANE - 1, 128, 128), BF),
            pltpu.VMEM((EARLY_STEPS * PLANE, 128, 128), BF),
            pltpu.VMEM(((8 - EARLY_STEPS) * PLANE, 128, 128), BF),
            pltpu.VMEM((EARLY * 128, 128), BF),
            pltpu.VMEM((EARLY * 128, 128), BF),
            pltpu.VMEM(((maxt - EARLY) * 128, 128), BF),
            pltpu.VMEM(((maxt - EARLY) * 128, 128), BF),
            pltpu.VMEM((CELLS, EARLY * 128), F32),
            pltpu.VMEM((CELLS, EARLY * 128), F32),
            pltpu.VMEM((ZN, CELLS, 128), F32),
            pltpu.VMEM((ZN, CELLS, 128), F32),
            pltpu.VMEM((CELLS, 128), F32),
            pltpu.VMEM((8, 128), jnp.int32),
            pltpu.VMEM((PLANE + 1, 8, 128), jnp.int32),
            pltpu.SMEM((PLANE + 1, 8, 128), jnp.int32),
            pltpu.VMEM((D, 3 * D), BF),
            pltpu.VMEM((D, D), BF),
            pltpu.VMEM((D, D), BF),
            pltpu.VMEM((2 * D, D), BF),
            dma((8,)),
            dma((4,)),
            dma,
            dma((7, 2)),
            dma((14,)),
            dma((16,)),
        ],
        compiler_params=pltpu.CompilerParams(
            collective_id=0, has_side_effects=True, vmem_limit_bytes=60 << 20
        ),
    )(
        tile_ids,
        key_mask,
        fact_cells,
        gain_col.reshape(1, D),
        gain_tile.reshape(1, D),
        tiles,
        w_qkv,
        w_col_out,
        w_query,
        w_tile_out,
    )


def solution(mesh):
    placed = (
        P("rows", "cols", None),
        P(),
        P(),
        P(),
        P(),
        P(),
        P(),
        P("rows", None, "cols", None),
        P("rows", None),
        P("rows", None),
    )
    return jax.shard_map(
        functools.partial(shards, rows_n=mesh.shape["rows"]),
        mesh=mesh,
        in_specs=placed,
        out_specs=P("rows", "cols", None),
        check_vma=False,
    )
```
